32 devices in a mesh: ctx: 8 (over y, x, core), head: 4 (over z).
Axes of the slice: x: 2, y: 2, z: 4, core: 2. Of those that a mesh axis runs over, the one named last changes fastest.
Arguments:
- queries: bfloat16 [8192, 6144], P(('ctx', 'head')), may hold values from -56 to 56
- key_rows: bfloat16 [8192, 6144], P(('ctx', 'head')), may hold values from -6 to 6
- value_rows: bfloat16 [8192, 6144], P(('ctx', 'head')), may hold values from -6 to 6
- key_tiles: int32 [48, 64, 18], P('head', 'ctx'), may hold values from -1 to 63, as said below
Outputs:
- attended: bfloat16 [8192, 6144], P(('ctx', 'head'))
The draws below stay inside these ranges and needn't reach their ends.
Inputs may be any that keep to these rules, and one draw needn't show every extreme that they name: In key_tiles[h, i] the live slots come first and name distinct tiles whose time slab differs from tile i's by at most one; the rest hold -1. Tile i itself and the tiles of the same cell one time slab before and after (where they exist) are always live. In every draw some head and tile have all 18 slots live.
All inputs are finite; a program needn't handle non-finite values.
Results may differ from the reference program's by a relative error of at most 0.0046.
Values may be sent and summed in bfloat16 or wider, within the bound.
No kernel may reach another device: no remote copies, remote signals or barrier semaphores. Data moves between devices by JAX's collectives and lax.ppermute only.
A program may use at most 128 MiB of HBM per device.

```python
import jax
import jax.numpy as jnp
from jax import lax

H = 48
HDIM = 128
D = 6144
TILE = 128
GY = 2
GX = 4
KT = 18
NTT = 8
NTILES = 64
TOKENS = 8192


def paired_rows(key):
    seed_base = jax.random.fold_in(key, 5)
    seed_query, seed_keys = jax.random.split(seed_base, 2)
    query_all = jnp.clip(jax.random.normal(seed_query, (TOKENS, D), jnp.float32), -6.0, 6.0)
    keys_all = jnp.clip(jax.random.normal(seed_keys, (TOKENS, D), jnp.float32), -6.0, 6.0)
    return (query_all, keys_all)


def draw_queries(key, part):
    return paired_rows(key)[0].astype(jnp.bfloat16)


def draw_key_rows(key, part):
    return paired_rows(key)[1].astype(jnp.bfloat16)


def draw_key_tiles(key, part):
    seed_base = jax.random.fold_in(key, 11)
    seed_y, seed_x, seed_wide = jax.random.split(seed_base, 3)
    reach_y = jax.random.randint(seed_y, (H,), 0, 2)
    reach_x = jax.random.randint(seed_x, (H,), 0, 2)
    wide_head = jax.random.randint(seed_wide, (), 0, H)
    reach_y = reach_y.at[wide_head].set(1)
    reach_x = reach_x.at[wide_head].set(1)
    cells = GY * GX
    tile_ids = jnp.arange(NTILES)
    slab_of = tile_ids // cells
    row_of = tile_ids % cells // GX
    col_of = tile_ids % GX
    offsets = jnp.arange(27)
    step_t = offsets // 9 - 1
    step_y = offsets // 3 % 3 - 1
    step_x = offsets % 3 - 1
    near_slab = slab_of[:, None] + step_t[None, :]
    near_row = row_of[:, None] + step_y[None, :]
    near_col = col_of[:, None] + step_x[None, :]
    inside = (near_slab >= 0) & (near_slab < NTT) & (near_row >= 0) & (near_row < GY) & (near_col >= 0) & (near_col < GX)
    within = (jnp.abs(step_y)[None, None, :] <= reach_y[:, None, None]) & (jnp.abs(step_x)[None, None, :] <= reach_x[:, None, None])
    usable = inside[None, :, :] & within
    target = near_slab * cells + near_row * GX + near_col
    ranking = jnp.where(usable, offsets[None, None, :], 27 + offsets[None, None, :])
    order_ids = jnp.argsort(ranking, axis=-1, stable=True)[..., :KT]
    chosen = jnp.take_along_axis(jnp.broadcast_to(target[None], usable.shape), order_ids, axis=-1)
    chosen_ok = jnp.take_along_axis(usable, order_ids, axis=-1)
    return jnp.where(chosen_ok, chosen, -1).astype(jnp.int32)


def level_of(own_key, dims, cuts, low, top_value):
    def one(dim, shards_of):
        steps = jax.random.uniform(jax.random.fold_in(jax.random.fold_in(own_key, 6), dim), (shards_of,), jnp.float32, low / len(cuts), top_value / len(cuts))
        return jnp.repeat(jnp.exp(steps), dims[dim] // shards_of).reshape((-1,) + (1,) * (len(dims) - dim - 1))

    level = one(*cuts[0])
    for cut in cuts[1:]:
        level = level * one(*cut)
    return level


def gaussian(own_key, dims, width, reach, pieces=(), held_as=jnp.bfloat16):
    values = jax.random.normal(own_key, dims, jnp.float32) * width
    if len(pieces) > 0:
        values = level_of(own_key, dims, pieces, -0.22, 0.18) * values
    return jnp.clip(values, min=-reach, max=reach).astype(held_as)


def setup_inputs(seed: int = 0) -> dict:
    splits = jax.random.split(jax.random.key(seed), 5)
    return {
        "queries": draw_queries(jax.random.fold_in(splits[4], 71), 0),
        "key_rows": draw_key_rows(jax.random.fold_in(splits[4], 71), 0),
        "value_rows": gaussian(splits[2], (TOKENS, D), 1.0, 6.0, ((0, 32),)),
        "key_tiles": draw_key_tiles(jax.random.fold_in(splits[4], 71), 0),
    }


def one_head(operands):
    head_query, head_keys, head_values, listed = operands
    is_live = listed >= 0
    safe_ids = jnp.where(is_live, listed, 0).astype(jnp.int32)
    picked_keys = head_keys[safe_ids].astype(jnp.float32)
    picked_values = head_values[safe_ids].astype(jnp.float32)
    scores = jnp.einsum("qtd,qksd->qtks", head_query.astype(jnp.float32), picked_keys, precision=lax.Precision.HIGHEST) * (HDIM ** -0.5)
    live_mask = is_live[:, None, :, None]
    scores = jnp.where(live_mask, scores, jnp.float32(-1e30))
    row_max = jnp.max(scores, axis=(2, 3), keepdims=True)
    weight = jnp.where(live_mask, jnp.exp(scores - row_max), jnp.float32(0.0))
    row_total = jnp.sum(weight, axis=(2, 3))
    probs = lax.optimization_barrier(weight.astype(jnp.bfloat16))
    numerator = jnp.einsum("qtks,qksd->qtd", probs.astype(jnp.float32), picked_values, precision=lax.Precision.HIGHEST)
    return (numerator / row_total[..., None]).astype(jnp.bfloat16)


def by_head(array):
    return array.reshape(NTILES, TILE, H, HDIM).transpose(2, 0, 1, 3)


def reference(queries, key_rows, value_rows, key_tiles):
    result = lax.map(one_head, (by_head(queries), by_head(key_rows), by_head(value_rows), key_tiles))
    return result.transpose(1, 2, 0, 3).reshape(TOKENS, H * HDIM)
```

```python
import functools

import jax
import jax.numpy as jnp
from jax import lax
from jax.experimental import pallas as pl
from jax.experimental.pallas import tpu as pltpu
from jax.sharding import PartitionSpec as P

HDIM = 128
TILE = 128
LOG2E = 1.4426950408889634
DEAD = 1e30
CHUNK_HEADS = 2


HBM = pl.BlockSpec(memory_space=pl.ANY)
SMEM = pl.BlockSpec(memory_space=pltpu.SMEM)


def run_copies(copies):
    for copy in copies:
        copy.start()
    for copy in copies:
        copy.wait()


def head_columns(first_head, width):
    return pl.ds(pl.multiple_of(first_head * HDIM, HDIM), width)


def pack_body(peers, heads_dev, first, width, place, *refs):
    arrays, (outs, (held, in_sems, out_sems)) = refs[:3], (refs[3 : 3 + peers - 1], refs[3 + peers - 1 :])
    me = place[0]
    loads = []
    for shift in range(1, peers):
        columns = head_columns(lax.rem(me + shift, peers) * heads_dev + first, width)
        loads.append(
            [
                pltpu.make_async_copy(
                    array.at[:, columns], held.at[shift - 1, which], in_sems.at[shift - 1, which]
                )
                for which, array in enumerate(arrays)
            ]
        )
    for group in loads:
        for copy in group:
            copy.start()
    stores = []
    for shift in range(1, peers):
        for copy in loads[shift - 1]:
            copy.wait()
        store = pltpu.make_async_copy(held.at[shift - 1], outs[shift - 1], out_sems.at[shift - 1])
        store.start()
        stores.append(store)
    for store in stores:
        store.wait()


def pack(place, arrays, peers, heads_dev, first, width):
    rows = arrays[0].shape[0]
    piece = jax.ShapeDtypeStruct((3, rows, width), jnp.bfloat16)
    moved = 3 * (peers - 1) * rows * width * 2
    return pl.pallas_call(
        functools.partial(pack_body, peers, heads_dev, first, width),
        out_shape=[piece] * (peers - 1),
        in_specs=[SMEM] + [HBM] * 3,
        out_specs=[HBM] * (peers - 1),
        scratch_shapes=[
            pltpu.VMEM((peers - 1, 3, rows, width), jnp.bfloat16),
            pltpu.SemaphoreType.DMA((peers - 1, 3)),
            pltpu.SemaphoreType.DMA((peers - 1,)),
        ],
        cost_estimate=pl.CostEstimate(flops=0, bytes_accessed=2 * moved, transcendentals=0),
        name="pack",
    )(place, *arrays)


def join_body(peers, heads_dev, first, width, place, key_rows, value_rows, *refs):
    pieces, (out, held, in_sems, out_sem) = refs[: peers - 1], refs[peers - 1 :]
    me = place[0]
    rows = key_rows.shape[0]
    own = head_columns(me * heads_dev + first, width)
    loads = []
    for which, array in enumerate((key_rows, value_rows)):
        loads.append(
            pltpu.make_async_copy(
                array.at[:, own], held.at[which, pl.ds(pl.multiple_of(me * rows, rows), rows)], in_sems.at[0, which]
            )
        )
        for shift in range(1, peers):
            source = lax.rem(me + peers - shift, peers)
            loads.append(
                pltpu.make_async_copy(
                    pieces[shift - 1].at[1 + which],
                    held.at[which, pl.ds(pl.multiple_of(source * rows, rows), rows)],
                    in_sems.at[shift, which],
                )
            )
    run_copies(loads)
    run_copies([pltpu.make_async_copy(held, out, out_sem)])


def join(place, key_rows, value_rows, pieces, heads_dev, first, width):
    peers = len(pieces) + 1
    rows = key_rows.shape[0]
    shape = (2, peers * rows, width)
    return pl.pallas_call(
        functools.partial(join_body, peers, heads_dev, first, width),
        out_shape=jax.ShapeDtypeStruct(shape, jnp.bfloat16),
        in_specs=[SMEM] + [HBM] * (2 + peers - 1),
        out_specs=HBM,
        scratch_shapes=[
            pltpu.VMEM(shape, jnp.bfloat16),
            pltpu.SemaphoreType.DMA((peers, 2)),
            pltpu.SemaphoreType.DMA,
        ],
        cost_estimate=pl.CostEstimate(flops=0, bytes_accessed=4 * peers * rows * width * 2, transcendentals=0),
        name="join",
    )(place, key_rows, value_rows, *pieces)


def attend_body(peers, heads_dev, first, width, slots, place, tiles, queries, *refs):
    pieces, refs = refs[: peers - 1], refs[peers - 1 :]
    sides, refs = refs[:3], refs[3:]
    outs, refs = refs[:peers], refs[peers:]
    q_held, kv_held, o_held, scores, peak, total, sums, q_sems, kv_sems, o_sems = refs
    me = place[0]
    rows = queries.shape[0]
    block = peers * rows
    q_tiles = block // TILE
    pairs = (slots + 1) // 2

    loads = [
        pltpu.make_async_copy(
            queries.at[:, head_columns(me * heads_dev + first, width)],
            q_held.at[pl.ds(pl.multiple_of(me * rows, rows), rows)],
            q_sems.at[0],
        )
    ]
    for shift in range(1, peers):
        source = lax.rem(me + peers - shift, peers)
        loads.append(
            pltpu.make_async_copy(
                pieces[shift - 1].at[0],
                q_held.at[pl.ds(pl.multiple_of(source * rows, rows), rows)],
                q_sems.at[shift],
            )
        )
    for side in range(3):
        loads.append(
            pltpu.make_async_copy(
                sides[side], kv_held.at[:, pl.ds(side * block, block)], kv_sems.at[side]
            )
        )
    run_copies(loads)

    factor = HDIM ** (-0.5) * LOG2E
    for head in range(width // HDIM):
        lanes = pl.ds(head * HDIM, HDIM)

        def listed(tile, slot):
            return tiles[head, tile * (2 * pairs + 1) + 1 + slot]

        def live(tile):
            return tiles[head, tile * (2 * pairs + 1)]

        def gathered(which, tile, pair):
            return jnp.concatenate(
                [
                    kv_held[which, pl.ds(pl.multiple_of(listed(tile, 2 * pair + half) * TILE, TILE), TILE), lanes]
                    for half in range(2)
                ],
                axis=0,
            )

        longest = live(0)
        for tile in range(1, q_tiles):
            longest = jnp.maximum(longest, live(tile))
        steps = (longest + 1) // 2

        peak[...] = jnp.full_like(peak, -jnp.inf)
        total[...] = jnp.zeros_like(total)
        sums[...] = jnp.zeros_like(sums)

        @pl.loop(0, steps)
        def _(pair):
            for tile in range(q_tiles):
                at = pl.ds(tile * TILE, TILE)
                score = lax.dot_general(
                    q_held[at, lanes],
                    gathered(0, tile, pair),
                    (((1,), (1,)), ((), ())),
                    preferred_element_type=jnp.float32,
                )
                scores[pair, at] = score
                peak[at] = jnp.maximum(peak[at], jnp.maximum(score[:, :TILE], score[:, TILE:]))

        for tile in range(q_tiles):
            at = pl.ds(tile * TILE, TILE)
            top = jnp.max(peak[at], axis=1, keepdims=True) * factor
            peak[at] = jnp.broadcast_to(top, (TILE, TILE))

        @pl.loop(0, steps)
        def _(pair):
            for tile in range(q_tiles):
                at = pl.ds(tile * TILE, TILE)
                top = peak[at]
                parts = []
                for half in range(2):
                    base = jnp.where(2 * pair + half < live(tile), top, DEAD)
                    parts.append(
                        jnp.exp2(scores[pair, at, pl.ds(half * TILE, TILE)] * factor - base)
                    )
                total[at] += parts[0] + parts[1]
                weight = jnp.concatenate(parts, axis=1).astype(jnp.bfloat16)
                sums[at] += jnp.dot(
                    weight, gathered(1, tile, pair), preferred_element_type=jnp.float32
                )

        for tile in range(q_tiles):
            at = pl.ds(tile * TILE, TILE)
            row_total = jnp.sum(total[at], axis=1, keepdims=True)
            o_held[at, lanes] = (sums[at] / row_total).astype(jnp.bfloat16)

    run_copies(
        [
            pltpu.make_async_copy(
                o_held.at[pl.ds(pl.multiple_of(lax.rem(me + shift, peers) * rows, rows), rows)],
                outs[shift],
                o_sems.at[shift],
            )
            for shift in range(peers)
        ]
    )


def attend(place, tiles, queries, pieces, sides, heads_dev, first, width, slots):
    peers = len(pieces) + 1
    rows = queries.shape[0]
    block = peers * rows
    pairs = (slots + 1) // 2
    work = (width // HDIM) * block * slots * TILE
    return pl.pallas_call(
        functools.partial(attend_body, peers, heads_dev, first, width, slots),
        out_shape=[jax.ShapeDtypeStruct((rows, width), jnp.bfloat16)] * peers,
        in_specs=[SMEM, SMEM] + [HBM] * (1 + peers - 1 + 3),
        out_specs=[HBM] * peers,
        scratch_shapes=[
            pltpu.VMEM((block, width), jnp.bfloat16),
            pltpu.VMEM((2, 3 * block, width), jnp.bfloat16),
            pltpu.VMEM((block, width), jnp.bfloat16),
            pltpu.VMEM((pairs, block, 2 * TILE), jnp.float32),
            pltpu.VMEM((block, TILE), jnp.float32),
            pltpu.VMEM((block, TILE), jnp.float32),
            pltpu.VMEM((block, HDIM), jnp.float32),
            pltpu.SemaphoreType.DMA((peers,)),
            pltpu.SemaphoreType.DMA((3,)),
            pltpu.SemaphoreType.DMA((peers,)),
        ],
        cost_estimate=pl.CostEstimate(
            flops=4 * work * HDIM, bytes_accessed=8 * block * width * 2, transcendentals=work
        ),
        name="attend",
    )(place, tiles, queries, *pieces, *sides)


def place_body(peers, heads_dev, first, width, aliased, place, *refs):
    pieces, refs = refs[:peers], refs[peers + aliased :]
    out, held, in_sems, out_sems = refs
    me = place[0]
    loads = [
        pltpu.make_async_copy(pieces[shift], held.at[shift], in_sems.at[shift]) for shift in range(peers)
    ]
    for copy in loads:
        copy.start()
    stores = []
    for shift in range(peers):
        source = lax.rem(me + peers - shift, peers)
        loads[shift].wait()
        store = pltpu.make_async_copy(
            held.at[shift], out.at[:, head_columns(source * heads_dev + first, width)], out_sems.at[shift]
        )
        store.start()
        stores.append(store)
    for store in stores:
        store.wait()


def place_columns(place, pieces, out, heads_dev, first, width, shape):
    peers = len(pieces)
    rows = shape[0]
    aliased = 0 if out is None else 1
    return pl.pallas_call(
        functools.partial(place_body, peers, heads_dev, first, width, aliased),
        out_shape=jax.ShapeDtypeStruct(shape, jnp.bfloat16),
        in_specs=[SMEM] + [HBM] * (peers + aliased),
        out_specs=HBM,
        input_output_aliases={1 + peers: 0} if aliased else {},
        scratch_shapes=[
            pltpu.VMEM((peers, rows, width), jnp.bfloat16),
            pltpu.SemaphoreType.DMA((peers,)),
            pltpu.SemaphoreType.DMA((peers,)),
        ],
        cost_estimate=pl.CostEstimate(flops=0, bytes_accessed=4 * peers * rows * width, transcendentals=0),
        name="place",
    )(place, *pieces, *(() if out is None else (out,)))


def around(array, axis, shift):
    count = lax.axis_size(axis)
    return lax.ppermute(array, axis, [(i, (i + shift) % count) for i in range(count)])


def along(array, axis, shift):
    count = lax.axis_size(axis)
    return lax.ppermute(array, axis, [(i, i + shift) for i in range(count) if 0 <= i + shift < count])


def shards(queries, key_rows, value_rows, key_tiles):
    peers = lax.axis_size("head")
    heads_dev, q_tiles, slots = key_tiles.shape
    group = CHUNK_HEADS if heads_dev % CHUNK_HEADS == 0 else 1
    width = group * HDIM
    chunks = range(0, heads_dev, group)
    place = lax.axis_index("head").astype(jnp.int32).reshape(1)

    pairs = (slots + 1) // 2
    tile_base = (lax.axis_index("ctx") - 1) * q_tiles
    is_live = key_tiles >= 0
    local_ids = jnp.where(is_live, key_tiles - tile_base, key_tiles[:, :, :1] - tile_base)
    counts = jnp.sum(is_live.astype(jnp.int32), axis=2, keepdims=True)
    filler = local_ids[:, :, :1]
    lists = jnp.concatenate([counts, local_ids] + [filler] * (2 * pairs - slots), axis=2)
    lists = lists.reshape(heads_dev, q_tiles * (2 * pairs + 1)).astype(jnp.int32)

    arrays = (queries, key_rows, value_rows)
    arrived = []
    for first in chunks:
        sent = pack(place, arrays, peers, heads_dev, first, width)
        arrived.append([around(piece, "head", shift + 1) for shift, piece in enumerate(sent)])
    out = None
    for index, first in enumerate(chunks):
        pieces = arrived[index]
        own = join(place, key_rows, value_rows, pieces, heads_dev, first, width)
        low = along(own, "ctx", 1)
        high = along(own, "ctx", -1)
        results = attend(
            place, lists[first : first + group], queries, pieces, (low, own, high), heads_dev, first, width, slots
        )
        back = [results[0]] + [around(results[shift], "head", shift) for shift in range(1, peers)]
        out = place_columns(place, back, out, heads_dev, first, width, queries.shape)
    return out


def solution(mesh):
    placed = (
        P(("ctx", "head"), None),
        P(("ctx", "head"), None),
        P(("ctx", "head"), None),
        P("head", "ctx", None),
    )
    return jax.shard_map(
        shards, mesh=mesh, in_specs=placed, out_specs=P(("ctx", "head"), None), check_vma=False
    )
```

```python
import functools

import jax
import jax.numpy as jnp
from jax import lax
from jax.experimental import pallas as pl
from jax.experimental.pallas import tpu as pltpu
from jax.sharding import PartitionSpec as P


HDIM = 128
TILE = 128
LOG2E = 1.4426950408889634
DEAD = 1e30
CHUNK_HEADS = 3
AHEAD = 2
VMEM_LIMIT = 67043328


HBM = pl.BlockSpec(memory_space=pl.ANY)
SMEM = pl.BlockSpec(memory_space=pltpu.SMEM)


def run_copies(copies):
    for copy in copies:
        copy.start()
    for copy in copies:
        copy.wait()


def head_columns(first_head, width):
    return pl.ds(pl.multiple_of(first_head * HDIM, HDIM), width)


def params():
    return pltpu.CompilerParams(vmem_limit_bytes=VMEM_LIMIT)


def pack_body(peers, heads_dev, chunks, place, *refs):
    sends = len(chunks) * (peers - 1)
    arrays, outs, held, (in_sems, out_sems) = refs[:3], refs[3 : 3 + sends], refs[3 + sends : -2], refs[-2:]
    me = place[0]
    loads = []
    for index, (first, group) in enumerate(chunks):
        for shift in range(1, peers):
            columns = head_columns(lax.rem(me + shift, peers) * heads_dev + first, group * HDIM)
            slot = index * (peers - 1) + shift - 1
            loads.append(
                [
                    pltpu.make_async_copy(
                        array.at[:, columns], held[index].at[shift - 1, which], in_sems.at[slot, which]
                    )
                    for which, array in enumerate(arrays)
                ]
            )
    for copies in loads:
        for copy in copies:
            copy.start()
    stores = []
    for slot, copies in enumerate(loads):
        for copy in copies:
            copy.wait()
        index, shift = divmod(slot, peers - 1)
        store = pltpu.make_async_copy(held[index].at[shift], outs[slot], out_sems.at[slot])
        store.start()
        stores.append(store)
    for store in stores:
        store.wait()


def pack(place, arrays, peers, heads_dev, chunks):
    rows = arrays[0].shape[0]
    outs = [
        jax.ShapeDtypeStruct((3, rows, group * HDIM), jnp.bfloat16) for _, group in chunks for _ in range(peers - 1)
    ]
    moved = sum(3 * (peers - 1) * rows * group * HDIM * 2 for _, group in chunks)
    results = pl.pallas_call(
        functools.partial(pack_body, peers, heads_dev, chunks),
        out_shape=outs,
        in_specs=[SMEM] + [HBM] * 3,
        out_specs=[HBM] * len(outs),
        scratch_shapes=[pltpu.VMEM((peers - 1, 3, rows, group * HDIM), jnp.bfloat16) for _, group in chunks]
        + [
            pltpu.SemaphoreType.DMA((len(outs), 3)),
            pltpu.SemaphoreType.DMA((len(outs),)),
        ],
        cost_estimate=pl.CostEstimate(flops=0, bytes_accessed=2 * moved, transcendentals=0),
        compiler_params=params(),
        name="pack",
    )(place, *arrays)
    return [results[i : i + peers - 1] for i in range(0, len(outs), peers - 1)]


def join_body(peers, heads_dev, first, width, place, key_rows, value_rows, *refs):
    pieces, (out, held, in_sems, out_sem) = refs[: peers - 1], refs[peers - 1 :]
    me = place[0]
    rows = key_rows.shape[0]
    own = head_columns(me * heads_dev + first, width)
    loads = []
    for which, array in enumerate((key_rows, value_rows)):
        loads.append(
            pltpu.make_async_copy(
                array.at[:, own], held.at[which, pl.ds(pl.multiple_of(me * rows, rows), rows)], in_sems.at[0, which]
            )
        )
        for shift in range(1, peers):
            source = lax.rem(me + peers - shift, peers)
            loads.append(
                pltpu.make_async_copy(
                    pieces[shift - 1].at[1 + which],
                    held.at[which, pl.ds(pl.multiple_of(source * rows, rows), rows)],
                    in_sems.at[shift, which],
                )
            )
    run_copies(loads)
    run_copies([pltpu.make_async_copy(held, out, out_sem)])


def join(place, key_rows, value_rows, pieces, heads_dev, first, width):
    peers = len(pieces) + 1
    rows = key_rows.shape[0]
    shape = (2, peers * rows, width)
    return pl.pallas_call(
        functools.partial(join_body, peers, heads_dev, first, width),
        out_shape=jax.ShapeDtypeStruct(shape, jnp.bfloat16),
        in_specs=[SMEM] + [HBM] * (2 + peers - 1),
        out_specs=HBM,
        scratch_shapes=[
            pltpu.VMEM(shape, jnp.bfloat16),
            pltpu.SemaphoreType.DMA((peers, 2)),
            pltpu.SemaphoreType.DMA,
        ],
        cost_estimate=pl.CostEstimate(flops=0, bytes_accessed=4 * peers * rows * width * 2, transcendentals=0),
        compiler_params=params(),
        name="join",
    )(place, key_rows, value_rows, *pieces)


def attend_body(peers, heads_dev, first, group, slots, place, tiles, queries, *refs):
    pieces, refs = refs[: peers - 1], refs[peers - 1 :]
    sides, refs = refs[:3], refs[3:]
    outs, refs = refs[:peers], refs[peers:]
    q_held, kv_held, o_held, scores, peak, total, sums, q_sems, kv_sems, o_sems = refs
    me = place[0]
    rows = queries.shape[0]
    block = peers * rows
    q_tiles = block // TILE
    pairs = (slots + 1) // 2
    entries = 2 * pairs + 1

    loads = []
    for head in range(group):
        lanes = pl.ds(head * HDIM, HDIM)
        copies = [
            pltpu.make_async_copy(
                queries.at[:, head_columns(me * heads_dev + first + head, HDIM)],
                q_held.at[head, pl.ds(pl.multiple_of(me * rows, rows), rows)],
                q_sems.at[head, 0],
            )
        ]
        for shift in range(1, peers):
            source = lax.rem(me + peers - shift, peers)
            copies.append(
                pltpu.make_async_copy(
                    pieces[shift - 1].at[0, :, lanes],
                    q_held.at[head, pl.ds(pl.multiple_of(source * rows, rows), rows)],
                    q_sems.at[head, shift],
                )
            )
        for which in range(2):
            for side in range(3):
                copies.append(
                    pltpu.make_async_copy(
                        sides[side].at[which, :, lanes],
                        kv_held.at[head, which, pl.ds(side * block, block)],
                        kv_sems.at[head, which, side],
                    )
                )
        loads.append((copies[: peers + 3], copies[peers + 3 :]))
    for early, late in loads:
        for copy in early + late:
            copy.start()

    factor = HDIM ** (-0.5) * LOG2E
    stores = []
    for head in range(group):
        lanes = pl.ds(head * HDIM, HDIM)

        def listed(tile, slot):
            return tiles[head, tile * entries + 1 + slot]

        def live(tile):
            return tiles[head, tile * entries]

        def gathered(which, tile, pair):
            return jnp.concatenate(
                [
                    kv_held[head, which, pl.ds(pl.multiple_of(listed(tile, 2 * pair + half) * TILE, TILE), TILE)]
                    for half in range(2)
                ],
                axis=0,
            )

        longest = live(0)
        for tile in range(1, q_tiles):
            longest = jnp.maximum(longest, live(tile))
        steps = (longest + 1) // 2

        peak[...] = jnp.full_like(peak, -jnp.inf)
        total[...] = jnp.zeros_like(total)
        sums[...] = jnp.zeros_like(sums)
        for copy in loads[head][0]:
            copy.wait()

        @pl.loop(0, steps)
        def _(pair):
            for tile in range(q_tiles):
                at = pl.ds(tile * TILE, TILE)
                score = lax.dot_general(
                    q_held[head, at],
                    gathered(0, tile, pair),
                    (((1,), (1,)), ((), ())),
                    preferred_element_type=jnp.float32,
                )
                scores[pair, at] = score
                peak[at] = jnp.maximum(peak[at], jnp.maximum(score[:, :TILE], score[:, TILE:]))

        for tile in range(q_tiles):
            at = pl.ds(tile * TILE, TILE)
            top = jnp.max(peak[at], axis=1, keepdims=True) * factor
            peak[at] = jnp.broadcast_to(top, (TILE, TILE))
        for copy in loads[head][1]:
            copy.wait()

        @pl.loop(0, steps)
        def _(pair):
            for tile in range(q_tiles):
                at = pl.ds(tile * TILE, TILE)
                top = peak[at]
                parts = []
                for half in range(2):
                    base = jnp.where(2 * pair + half < live(tile), top, DEAD)
                    parts.append(
                        jnp.exp2(scores[pair, at, pl.ds(half * TILE, TILE)] * factor - base)
                    )
                total[at] += parts[0] + parts[1]
                weight = jnp.concatenate(parts, axis=1).astype(jnp.bfloat16)
                sums[at] += jnp.dot(
                    weight, gathered(1, tile, pair), preferred_element_type=jnp.float32
                )

        for tile in range(q_tiles):
            at = pl.ds(tile * TILE, TILE)
            row_total = jnp.sum(total[at], axis=1, keepdims=True)
            o_held[head, at] = (sums[at] / row_total).astype(jnp.bfloat16)
        for shift in range(peers):
            target = lax.rem(me + shift, peers)
            store = pltpu.make_async_copy(
                o_held.at[head, pl.ds(pl.multiple_of(target * rows, rows), rows)],
                outs[shift].at[:, lanes],
                o_sems.at[head, shift],
            )
            store.start()
            stores.append(store)
    for store in stores:
        store.wait()


def attend(place, tiles, queries, pieces, sides, heads_dev, first, group, slots):
    peers = len(pieces) + 1
    rows = queries.shape[0]
    block = peers * rows
    width = group * HDIM
    pairs = (slots + 1) // 2
    work = group * block * slots * TILE
    return pl.pallas_call(
        functools.partial(attend_body, peers, heads_dev, first, group, slots),
        out_shape=[jax.ShapeDtypeStruct((rows, width), jnp.bfloat16)] * peers,
        in_specs=[SMEM, SMEM] + [HBM] * (1 + peers - 1 + 3),
        out_specs=[HBM] * peers,
        scratch_shapes=[
            pltpu.VMEM((group, block, HDIM), jnp.bfloat16),
            pltpu.VMEM((group, 2, 3 * block, HDIM), jnp.bfloat16),
            pltpu.VMEM((group, block, HDIM), jnp.bfloat16),
            pltpu.VMEM((pairs, block, 2 * TILE), jnp.float32),
            pltpu.VMEM((block, TILE), jnp.float32),
            pltpu.VMEM((block, TILE), jnp.float32),
            pltpu.VMEM((block, HDIM), jnp.float32),
            pltpu.SemaphoreType.DMA((group, peers)),
            pltpu.SemaphoreType.DMA((group, 2, 3)),
            pltpu.SemaphoreType.DMA((group, peers)),
        ],
        cost_estimate=pl.CostEstimate(
            flops=4 * work * HDIM, bytes_accessed=8 * block * width * 2, transcendentals=work
        ),
        compiler_params=params(),
        name="attend",
    )(place, tiles, queries, *pieces, *sides)


def place_body(peers, heads_dev, chunks, aliased, place, *refs):
    count = len(chunks) * peers
    pieces, out, held, (in_sems, out_sems) = refs[:count], refs[count + aliased], refs[count + aliased + 1 : -2], refs[-2:]
    me = place[0]
    loads, stores = [], []
    for index, (first, group) in enumerate(chunks):
        for shift in range(peers):
            slot = index * peers + shift
            source = lax.rem(me + peers - shift, peers)
            loads.append(pltpu.make_async_copy(pieces[slot], held[index].at[shift], in_sems.at[slot]))
            stores.append(
                pltpu.make_async_copy(
                    held[index].at[shift],
                    out.at[:, head_columns(source * heads_dev + first, group * HDIM)],
                    out_sems.at[slot],
                )
            )
    for load in loads:
        load.start()
    for load, store in zip(loads, stores):
        load.wait()
        store.start()
    for store in stores:
        store.wait()


def place_columns(place, pieces, out, heads_dev, chunks, shape):
    peers = len(pieces) // len(chunks)
    rows = shape[0]
    aliased = 0 if out is None else 1
    moved = sum(2 * peers * rows * group * HDIM * 2 for _, group in chunks)
    return pl.pallas_call(
        functools.partial(place_body, peers, heads_dev, chunks, aliased),
        out_shape=jax.ShapeDtypeStruct(shape, jnp.bfloat16),
        in_specs=[SMEM] + [HBM] * (len(pieces) + aliased),
        out_specs=HBM,
        input_output_aliases={1 + len(pieces): 0} if aliased else {},
        scratch_shapes=[pltpu.VMEM((peers, rows, group * HDIM), jnp.bfloat16) for _, group in chunks]
        + [
            pltpu.SemaphoreType.DMA((len(pieces),)),
            pltpu.SemaphoreType.DMA((len(pieces),)),
        ],
        cost_estimate=pl.CostEstimate(flops=0, bytes_accessed=moved, transcendentals=0),
        compiler_params=params(),
        name="place",
    )(place, *pieces, *(() if out is None else (out,)))


def groups_of(heads_dev):
    groups, first = [], 0
    while first < heads_dev:
        left = heads_dev - first
        group = min(CHUNK_HEADS, (left + 1) // 2)
        groups.append((first, group))
        first += group
    return groups


def around(array, axis, shift):
    count = lax.axis_size(axis)
    return lax.ppermute(array, axis, [(i, (i + shift) % count) for i in range(count)])


def along(array, axis, shift):
    count = lax.axis_size(axis)
    return lax.ppermute(array, axis, [(i, i + shift) for i in range(count) if 0 <= i + shift < count])


def after(place, values):
    return lax.optimization_barrier((place, values))[0]


def shards(queries, key_rows, value_rows, key_tiles):
    peers = lax.axis_size("head")
    heads_dev, q_tiles, slots = key_tiles.shape
    chunks = groups_of(heads_dev)
    place = lax.axis_index("head").astype(jnp.int32).reshape(1)

    pairs = (slots + 1) // 2
    tile_base = (lax.axis_index("ctx") - 1) * q_tiles
    is_live = key_tiles >= 0
    local_ids = jnp.where(is_live, key_tiles - tile_base, key_tiles[:, :, :1] - tile_base)
    counts = jnp.sum(is_live.astype(jnp.int32), axis=2, keepdims=True)
    filler = local_ids[:, :, :1]
    lists = jnp.concatenate([counts, local_ids] + [filler] * (2 * pairs - slots), axis=2)
    lists = lists.reshape(heads_dev, q_tiles * (2 * pairs + 1)).astype(jnp.int32)

    arrays = (queries, key_rows, value_rows)
    arrived, joined, attended = {}, {}, {}

    def moved(array, axis, shift):
        return around(array, axis, shift) if axis == "head" else along(array, axis, shift)

    for kind, index in kernel_order(len(chunks)):
        if kind == "pack":
            results = pack(place, arrays, peers, heads_dev, [chunks[index]])
        elif kind == "join":
            first, group = chunks[index]
            results = join(place, key_rows, value_rows, arrived[index], heads_dev, first, group * HDIM)
        else:
            first, group = chunks[index]
            results = attend(
                place, lists[first : first + group], queries, arrived[index], joined[index], heads_dev, first,
                group, slots,
            )
        if kind == "pack":
            arrived[index] = [moved(results[0][shift - 1], "head", shift) for shift in range(1, peers)]
        elif kind == "join":
            low, high = (moved(results, "ctx", side) for side in (1, -1))
            joined[index] = (low, results, high)
        else:
            attended[index] = [results[0]] + [moved(results[shift], "head", shift) for shift in range(1, peers)]
        place = after(place, results)
    out = None
    if len(chunks) > 1:
        pieces = [piece for index in range(len(chunks) - 1) for piece in attended[index]]
        out = place_columns(place, pieces, out, heads_dev, chunks[:-1], queries.shape)
    return place_columns(place, attended[len(chunks) - 1], out, heads_dev, chunks[-1:], queries.shape)


def kernel_order(count):
    order = [("pack", index) for index in range(min(AHEAD, count))]
    for step in range(count + 1):
        if step < count:
            order.append(("join", step))
        if step + AHEAD < count:
            order.append(("pack", step + AHEAD))
        if step >= 1:
            order.append(("attend", step - 1))
    return order


def solution(mesh):
    placed = (
        P(("ctx", "head"), None),
        P(("ctx", "head"), None),
        P(("ctx", "head"), None),
        P("head", "ctx", None),
    )
    return jax.shard_map(
        shards, mesh=mesh, in_specs=placed, out_specs=P(("ctx", "head"), None), check_vma=False
    )
```

```python
import functools
from typing import NamedTuple

import jax
import jax.numpy as jnp
from jax import lax
from jax.experimental import pallas as pl
from jax.experimental.pallas import tpu as pltpu
from jax.sharding import PartitionSpec as P


HDIM = 128
TILE = 128
LOG2E = 1.4426950408889634
DEAD = 1e30
AHEAD = 2
VMEM_LIMIT = 67043328
LANES = 128
WITHIN = 64
WIDE_HEADS = 3
NARROW_HEADS = 5


HBM = pl.BlockSpec(memory_space=pl.ANY)
SMEM = pl.BlockSpec(memory_space=pltpu.SMEM)


def run_copies(copies):
    for copy in copies:
        copy.start()
    for copy in copies:
        copy.wait()


def head_columns(head):
    return pl.ds(pl.multiple_of(head * HDIM, HDIM), HDIM)


def lanes_of(index):
    return pl.ds(index * HDIM, HDIM) if isinstance(index, int) else pl.ds(pl.multiple_of(index * HDIM, HDIM), HDIM)


def params():
    return pltpu.CompilerParams(vmem_limit_bytes=VMEM_LIMIT)


class Group(NamedTuple):
    peers: int
    base: int
    heads: int

    def head(self, order, member, index):
        return order[self.base + index * self.peers + member]


def pack_body(groups, place, order, *refs):
    sends = sum(group.peers - 1 for group in groups)
    arrays, outs, held, (in_sems, out_sems) = refs[:3], refs[3 : 3 + sends], refs[3 + sends : -2], refs[-2:]
    loads, stores, block = [], [], 0
    for number, group in enumerate(groups):
        me = lax.rem(place[0], group.peers)
        for shift in range(1, group.peers):
            member = lax.rem(me + shift, group.peers)
            copies = []
            for index in range(group.heads):
                columns = head_columns(group.head(order, member, index))
                for which, array in enumerate(arrays):
                    copies.append(
                        pltpu.make_async_copy(
                            array.at[:, columns],
                            held[number].at[shift - 1, which, :, lanes_of(index)],
                            in_sems.at[block],
                        )
                    )
                    block += 1
            sent = len(loads)
            loads.append(copies)
            stores.append(pltpu.make_async_copy(held[number].at[shift - 1], outs[sent], out_sems.at[sent]))
    for copies in loads:
        for copy in copies:
            copy.start()
    for copies, store in zip(loads, stores):
        for copy in copies:
            copy.wait()
        store.start()
    for store in stores:
        store.wait()


def pack(groups, place, order, arrays):
    rows = arrays[0].shape[0]
    outs = [
        jax.ShapeDtypeStruct((3, rows, group.heads * HDIM), jnp.bfloat16)
        for group in groups
        for _ in range(group.peers - 1)
    ]
    blocks = sum(3 * (group.peers - 1) * group.heads for group in groups)
    results = pl.pallas_call(
        functools.partial(pack_body, groups),
        out_shape=outs,
        in_specs=[SMEM, SMEM] + [HBM] * 3,
        out_specs=[HBM] * len(outs),
        scratch_shapes=[pltpu.VMEM((group.peers - 1, 3, rows, group.heads * HDIM), jnp.bfloat16) for group in groups]
        + [pltpu.SemaphoreType.DMA((blocks,)), pltpu.SemaphoreType.DMA((len(outs),))],
        cost_estimate=pl.CostEstimate(flops=0, bytes_accessed=4 * blocks * rows * HDIM, transcendentals=0),
        compiler_params=params(),
        name="pack",
    )(place, order, *arrays)
    sent = []
    for group in groups:
        sent.append(results[: group.peers - 1])
        results = results[group.peers - 1 :]
    return sent


def rows_of(member, rows):
    return pl.ds(pl.multiple_of(member * rows, rows), rows)


def join_body(group, place, order, key_rows, value_rows, *refs):
    peers = group.peers
    pieces, (out, held, own_sems, in_sems, out_sem) = refs[: peers - 1], refs[peers - 1 :]
    me = lax.rem(place[0], peers)
    rows = key_rows.shape[0]
    loads = []
    for which, array in enumerate((key_rows, value_rows)):
        for index in range(group.heads):
            loads.append(
                pltpu.make_async_copy(
                    array.at[:, head_columns(group.head(order, me, index))],
                    held.at[which, rows_of(me, rows), lanes_of(index)],
                    own_sems.at[which, index],
                )
            )
        for shift in range(1, peers):
            source = lax.rem(me + peers - shift, peers)
            loads.append(
                pltpu.make_async_copy(
                    pieces[shift - 1].at[1 + which], held.at[which, rows_of(source, rows)], in_sems.at[shift, which]
                )
            )
    run_copies(loads)
    run_copies([pltpu.make_async_copy(held, out, out_sem)])


def join(group, place, order, key_rows, value_rows, pieces):
    peers, rows = group.peers, key_rows.shape[0]
    shape = (2, peers * rows, group.heads * HDIM)
    return pl.pallas_call(
        functools.partial(join_body, group),
        out_shape=jax.ShapeDtypeStruct(shape, jnp.bfloat16),
        in_specs=[SMEM, SMEM] + [HBM] * (2 + peers - 1),
        out_specs=HBM,
        scratch_shapes=[
            pltpu.VMEM(shape, jnp.bfloat16),
            pltpu.SemaphoreType.DMA((2, group.heads)),
            pltpu.SemaphoreType.DMA((peers, 2)),
            pltpu.SemaphoreType.DMA,
        ],
        cost_estimate=pl.CostEstimate(flops=0, bytes_accessed=4 * shape[0] * shape[1] * shape[2], transcendentals=0),
        compiler_params=params(),
        name="join",
    )(place, order, key_rows, value_rows, *pieces)


def attend_body(group, column, place, order, lists, queries, *refs):
    peers, heads = group.peers, group.heads
    pieces, refs = refs[: peers - 1], refs[peers - 1 :]
    sides, refs = refs[:3], refs[3:]
    outs, refs = refs[:peers], refs[peers:]
    tiles, q_held, kv_held, o_held, scores, peak, total, sums, t_sems, own_sems, q_sems, kv_sems, o_sems = refs
    me = lax.rem(place[0], peers)
    rows = queries.shape[0]
    block = peers * rows
    q_tiles = block // TILE
    first_row = (place[0] // peers) * q_tiles

    def list_copy(head):
        return pltpu.make_async_copy(lists.at[group.head(order, me, head)], tiles.at[head], t_sems.at[head])

    def early(head):
        copies = [
            pltpu.make_async_copy(
                queries.at[:, head_columns(group.head(order, me, head))],
                q_held.at[head, rows_of(me, rows)],
                own_sems.at[head],
            )
        ]
        for shift in range(1, peers):
            source = lax.rem(me + peers - shift, peers)
            copies.append(
                pltpu.make_async_copy(
                    pieces[shift - 1].at[0, :, lanes_of(head)],
                    q_held.at[head, rows_of(source, rows)],
                    q_sems.at[head, shift],
                )
            )
        return copies + sides_of(head, 0)

    def sides_of(head, which):
        return [
            pltpu.make_async_copy(
                sides[side].at[which, :, lanes_of(head)],
                kv_held.at[head, which, pl.ds(side * block, block)],
                kv_sems.at[head, which, side],
            )
            for side in range(3)
        ]

    def back(head):
        return [
            pltpu.make_async_copy(
                o_held.at[head, rows_of(lax.rem(me + shift, peers), rows)],
                outs[shift].at[:, lanes_of(head)],
                o_sems.at[head, shift],
            )
            for shift in range(peers)
        ]

    for head in range(heads):
        for copy in [list_copy(head)] + early(head) + sides_of(head, 1):
            copy.start()

    factor = HDIM ** (-0.5) * LOG2E

    @pl.loop(0, heads)
    def _(head):
        def listed(tile, slot):
            return tiles[head, first_row + tile, column + 1 + slot]

        def live(tile):
            return tiles[head, first_row + tile, column]

        def gathered(which, tile, pair):
            return jnp.concatenate(
                [
                    kv_held[head, which, pl.ds(pl.multiple_of(listed(tile, 2 * pair + half) * TILE, TILE), TILE)]
                    for half in range(2)
                ],
                axis=0,
            )

        list_copy(head).wait()
        longest = live(0)
        for tile in range(1, q_tiles):
            longest = jnp.maximum(longest, live(tile))
        steps = (longest + 1) // 2

        peak[...] = jnp.full_like(peak, -jnp.inf)
        total[...] = jnp.zeros_like(total)
        sums[...] = jnp.zeros_like(sums)
        for copy in early(head):
            copy.wait()

        @pl.loop(0, steps)
        def _(pair):
            for tile in range(q_tiles):
                at = pl.ds(tile * TILE, TILE)
                score = lax.dot_general(
                    q_held[head, at],
                    gathered(0, tile, pair),
                    (((1,), (1,)), ((), ())),
                    preferred_element_type=jnp.float32,
                )
                scores[pair, at] = score
                peak[at] = jnp.maximum(peak[at], jnp.maximum(score[:, :TILE], score[:, TILE:]))

        for tile in range(q_tiles):
            at = pl.ds(tile * TILE, TILE)
            top = jnp.max(peak[at], axis=1, keepdims=True) * factor
            peak[at] = jnp.broadcast_to(top, (TILE, TILE))
        for copy in sides_of(head, 1):
            copy.wait()

        @pl.loop(0, steps)
        def _(pair):
            for tile in range(q_tiles):
                at = pl.ds(tile * TILE, TILE)
                top = peak[at]
                parts = []
                for half in range(2):
                    base = jnp.where(2 * pair + half < live(tile), top, DEAD)
                    parts.append(
                        jnp.exp2(scores[pair, at, pl.ds(half * TILE, TILE)] * factor - base)
                    )
                total[at] += parts[0] + parts[1]
                weight = jnp.concatenate(parts, axis=1).astype(jnp.bfloat16)
                sums[at] += jnp.dot(
                    weight, gathered(1, tile, pair), preferred_element_type=jnp.float32
                )

        for tile in range(q_tiles):
            at = pl.ds(tile * TILE, TILE)
            row_total = jnp.sum(total[at], axis=1, keepdims=True)
            o_held[head, at] = (sums[at] / row_total).astype(jnp.bfloat16)
        for copy in back(head):
            copy.start()

    for head in range(heads):
        for copy in back(head):
            copy.wait()


def attend(group, column, slots, place, order, lists, queries, pieces, sides):
    peers, heads = group.peers, group.heads
    rows = queries.shape[0]
    block = peers * rows
    width = heads * HDIM
    pairs = (slots + 1) // 2
    work = heads * block * slots * TILE
    return pl.pallas_call(
        functools.partial(attend_body, group, column),
        out_shape=[jax.ShapeDtypeStruct((rows, width), jnp.bfloat16)] * peers,
        in_specs=[SMEM, SMEM] + [HBM] * (2 + peers - 1 + 3),
        out_specs=[HBM] * peers,
        scratch_shapes=[
            pltpu.SMEM((heads,) + lists.shape[1:], jnp.int32),
            pltpu.VMEM((heads, block, HDIM), jnp.bfloat16),
            pltpu.VMEM((heads, 2, 3 * block, HDIM), jnp.bfloat16),
            pltpu.VMEM((heads, block, HDIM), jnp.bfloat16),
            pltpu.VMEM((pairs, block, 2 * TILE), jnp.float32),
            pltpu.VMEM((block, TILE), jnp.float32),
            pltpu.VMEM((block, TILE), jnp.float32),
            pltpu.VMEM((block, HDIM), jnp.float32),
            pltpu.SemaphoreType.DMA((heads,)),
            pltpu.SemaphoreType.DMA((heads,)),
            pltpu.SemaphoreType.DMA((heads, peers)),
            pltpu.SemaphoreType.DMA((heads, 2, 3)),
            pltpu.SemaphoreType.DMA((heads, peers)),
        ],
        cost_estimate=pl.CostEstimate(
            flops=4 * work * HDIM, bytes_accessed=8 * block * width * 2, transcendentals=work
        ),
        compiler_params=params(),
        name="attend",
    )(place, order, lists, queries, *pieces, *sides)


def place_body(groups, aliased, place, order, *refs):
    count = sum(group.peers for group in groups)
    pieces, out, held, (in_sems, out_sems) = refs[:count], refs[count + aliased], refs[count + aliased + 1 : -2], refs[-2:]
    loads, stores = [], []
    piece, block = 0, 0
    for number, group in enumerate(groups):
        me = lax.rem(place[0], group.peers)
        for shift in range(group.peers):
            source = lax.rem(me + group.peers - shift, group.peers)
            loads.append(pltpu.make_async_copy(pieces[piece], held[number].at[shift], in_sems.at[piece]))
            copies = []
            for index in range(group.heads):
                copies.append(
                    pltpu.make_async_copy(
                        held[number].at[shift, :, lanes_of(index)],
                        out.at[:, head_columns(group.head(order, source, index))],
                        out_sems.at[block],
                    )
                )
                block += 1
            stores.append(copies)
            piece += 1
    for load in loads:
        load.start()
    for load, copies in zip(loads, stores):
        load.wait()
        for copy in copies:
            copy.start()
    for copies in stores:
        for copy in copies:
            copy.wait()


def place_columns(groups, place, order, pieces, out, shape):
    rows = shape[0]
    aliased = 0 if out is None else 1
    blocks = sum(group.peers * group.heads for group in groups)
    return pl.pallas_call(
        functools.partial(place_body, groups, aliased),
        out_shape=jax.ShapeDtypeStruct(shape, jnp.bfloat16),
        in_specs=[SMEM, SMEM] + [HBM] * (len(pieces) + aliased),
        out_specs=HBM,
        input_output_aliases={2 + len(pieces): 0} if aliased else {},
        scratch_shapes=[pltpu.VMEM((group.peers, rows, group.heads * HDIM), jnp.bfloat16) for group in groups]
        + [
            pltpu.SemaphoreType.DMA((len(pieces),)),
            pltpu.SemaphoreType.DMA((blocks,)),
        ],
        cost_estimate=pl.CostEstimate(flops=0, bytes_accessed=4 * blocks * rows * HDIM, transcendentals=0),
        compiler_params=params(),
        name="place",
    )(place, order, *pieces, *(() if out is None else (out,)))


def around(array, peers, shift):
    count = lax.axis_size("head")
    moves = [(i, i // peers * peers + (i + shift) % peers) for i in range(count)]
    return lax.ppermute(array, "head", moves)


def along(array, shift):
    count = lax.axis_size("ctx")
    return lax.ppermute(array, "ctx", [(i, i + shift) for i in range(count) if 0 <= i + shift < count])


def after(place, values):
    return lax.optimization_barrier((place, values))[0]


def shares(heads, most):
    count = -(-heads // most)
    parts = [heads // count + (i < heads % count) for i in range(count)] if heads else []
    if count > 2 and parts[-1] > 1 and parts[0] == parts[-1]:
        parts[1], parts[-1] = parts[1] + 1, parts[-1] - 1
    return parts


def plan(wide, heads_dev, peers):
    half = peers // 2
    base, wides, narrows = 0, [], []
    for heads in shares(wide, WIDE_HEADS):
        wides.append(Group(peers, base, heads))
        base += peers * heads
    for heads in shares((heads_dev - wide) * (peers // half), NARROW_HEADS):
        narrows.append(Group(half, base, heads))
        base += half * heads
    mixed = []
    while wides or narrows:
        mixed += narrows[:1] + wides[:1]
        wides, narrows = wides[1:], narrows[1:]
    return mixed


def widths(heads_dev):
    return sorted({-(-heads_dev // 2), -(-2 * heads_dev // 3), heads_dev})


def list_rows(key_tiles):
    _, cells, slots = key_tiles.shape
    padded = slots + slots % 2
    is_live = key_tiles >= 0
    base = (lax.axis_index("ctx") - 1) * cells
    local_ids = jnp.where(is_live, key_tiles, key_tiles[:, :, :1]) - base
    counts = jnp.sum(is_live.astype(jnp.int32), axis=2, keepdims=True)
    half = cells // 2
    own_half = (jnp.arange(cells, dtype=jnp.int32) // half * half)[None, :, None]
    half_ids = local_ids // cells * half + local_ids % cells - own_half

    def row(ids, width):
        ids = jnp.pad(ids, ((0, 0), (0, 0), (0, padded - slots)))
        ids = jnp.concatenate([counts, ids], axis=2)
        return jnp.pad(ids, ((0, 0), (0, 0), (0, width - ids.shape[2])))

    return jnp.concatenate([row(local_ids, WITHIN), row(half_ids, LANES - WITHIN)], axis=2).astype(jnp.int32)


def sorted_heads(key_tiles):
    heads_dev, cells, _ = key_tiles.shape
    half = cells // 2
    is_live = key_tiles >= 0
    tile_half = (jnp.arange(cells, dtype=jnp.int32) // half)[None, :, None]
    crosses = jnp.any(is_live & (key_tiles % cells // half != tile_half), axis=(1, 2))
    longest = jnp.max(jnp.sum(is_live.astype(jnp.int32), axis=2), axis=1)
    mine = crosses.astype(jnp.int32) * LANES + longest
    tokens, peers = lax.axis_size("ctx"), lax.axis_size("head")
    spread = jnp.broadcast_to(mine[None], (tokens * peers, heads_dev))
    every = lax.all_to_all(spread, ("ctx", "head"), split_axis=0, concat_axis=0, tiled=True)
    score = jnp.max(every.reshape(tokens, peers * heads_dev), axis=0)
    index = jnp.arange(peers * heads_dev, dtype=jnp.int32)
    ahead = (score[None, :] > score[:, None]) | ((score[None, :] == score[:, None]) & (index[None, :] < index[:, None]))
    rank = jnp.sum(ahead.astype(jnp.int32), axis=1)
    order = jnp.sum(jnp.where(rank[None, :] == index[:, None], index[None, :], 0), axis=1)
    return order.astype(jnp.int32), jnp.sum((score >= LANES).astype(jnp.int32))


def pipeline(groups, place, order, queries, key_rows, value_rows, key_tiles):
    slots = key_tiles.shape[2]
    arrays = (queries, key_rows, value_rows)
    packed, arrived, joined, attended = {}, {}, {}, {}

    def send(index, pieces):
        arrived[index] = [
            around(pieces[shift - 1], groups[index].peers, shift)
            for shift in range(1, groups[index].peers)
        ]

    for kind, index in kernel_order(len(groups)):
        if kind == "join" and index == 0:
            rows = list_rows(after(key_tiles, place))
            lists = gather_heads(rows)
        group = groups[index]
        peers = group.peers
        if kind == "pack":
            results = pack(groups[index : index + 1] if index == 0 else groups[1:], place, order, arrays)
        elif kind == "join":
            results = join(group, place, order, key_rows, value_rows, arrived[index])
        else:
            column = 0 if peers == lax.axis_size("head") else WITHIN
            results = attend(
                group, column, slots, place, order, lists, queries, arrived[index], joined[index]
            )
        if kind == "pack":
            packed.update(zip(range(index, len(groups)), results))
            for ahead in range(index, min(AHEAD, index + 1)):
                send(ahead, packed[ahead])
        elif kind == "join":
            low, high = (along(results, side) for side in (1, -1))
            joined[index] = (low, results, high)
            if index + AHEAD < len(groups):
                send(index + AHEAD, after(packed[index + AHEAD], results))
        else:
            attended[index] = [results[0]] + [around(results[shift], peers, shift) for shift in range(1, peers)]
        place = after(place, results)
    out = None
    last = len(groups) - 1
    if last:
        pieces = [piece for index in range(last) for piece in attended[index]]
        out = place_columns(groups[:-1], place, order, pieces, out, queries.shape)
    return place_columns(groups[-1:], place, order, attended[last], out, queries.shape)


def gather_heads(rows):
    count = lax.axis_size("head")
    spread = jnp.broadcast_to(rows[None], (count,) + rows.shape)
    every = lax.all_to_all(spread, "head", split_axis=0, concat_axis=0, tiled=True)
    return every.reshape((-1,) + rows.shape[1:])


def plans(heads_dev, peers):
    return [plan(wide, heads_dev, peers) for wide in widths(heads_dev)]


def shards(queries, key_rows, value_rows, key_tiles):
    peers = lax.axis_size("head")
    heads_dev = key_tiles.shape[0]
    place = lax.axis_index("head").astype(jnp.int32).reshape(1)
    order, crossing = sorted_heads(key_tiles)
    which = jnp.int32(0)
    for wide in widths(heads_dev)[:-1]:
        which = which + (crossing > wide * peers).astype(jnp.int32)
    branches = [functools.partial(pipeline, groups) for groups in plans(heads_dev, peers)]
    return lax.switch(which, branches, place, order, queries, key_rows, value_rows, key_tiles)


def kernel_order(count):
    order = [("pack", index) for index in range(min(2, count))]
    for step in range(count + 1):
        if step < count:
            order.append(("join", step))
        if step >= 1:
            order.append(("attend", step - 1))
    return order


def solution(mesh):
    placed = (
        P(("ctx", "head"), None),
        P(("ctx", "head"), None),
        P(("ctx", "head"), None),
        P("head", "ctx", None),
    )
    return jax.shard_map(
        shards, mesh=mesh, in_specs=placed, out_specs=P(("ctx", "head"), None), check_vma=False
    )
```

```python
import functools
from typing import NamedTuple

import jax
import jax.numpy as jnp
from jax import lax
from jax.experimental import pallas as pl
from jax.experimental.pallas import tpu as pltpu
from jax.sharding import PartitionSpec as P


HDIM = 128
TILE = 128
LOG2E = 1.4426950408889634
DEAD = 1e30
AHEAD = 2
VMEM_LIMIT = 67043328
LANES = 128
WITHIN = 32
WIDE_HEADS = 3
NARROW_HEADS = 5


HBM = pl.BlockSpec(memory_space=pl.ANY)
SMEM = pl.BlockSpec(memory_space=pltpu.SMEM)


def run_copies(copies):
    for copy in copies:
        copy.start()
    for copy in copies:
        copy.wait()


def head_columns(head):
    return pl.ds(pl.multiple_of(head * HDIM, HDIM), HDIM)


def lanes_of(index):
    return pl.ds(index * HDIM, HDIM) if isinstance(index, int) else pl.ds(pl.multiple_of(index * HDIM, HDIM), HDIM)


def params():
    return pltpu.CompilerParams(vmem_limit_bytes=VMEM_LIMIT)


class Group(NamedTuple):
    peers: int
    base: int
    heads: int

    def head(self, order, member, index):
        return order[self.base + index * self.peers + member]


def pack_body(groups, place, order, *refs):
    sends = sum(group.peers - 1 for group in groups)
    arrays, outs, held, (in_sems, out_sems) = refs[:3], refs[3 : 3 + sends], refs[3 + sends : -2], refs[-2:]
    loads, stores, block = [], [], 0
    for number, group in enumerate(groups):
        me = lax.rem(place[0], group.peers)
        for shift in range(1, group.peers):
            member = lax.rem(me + shift, group.peers)
            copies = []
            for index in range(group.heads):
                columns = head_columns(group.head(order, member, index))
                for which, array in enumerate(arrays):
                    copies.append(
                        pltpu.make_async_copy(
                            array.at[:, columns],
                            held[number].at[shift - 1, which, :, lanes_of(index)],
                            in_sems.at[block],
                        )
                    )
                    block += 1
            sent = len(loads)
            loads.append(copies)
            stores.append(pltpu.make_async_copy(held[number].at[shift - 1], outs[sent], out_sems.at[sent]))
    for copies in loads:
        for copy in copies:
            copy.start()
    for copies, store in zip(loads, stores):
        for copy in copies:
            copy.wait()
        store.start()
    for store in stores:
        store.wait()


def pack(groups, place, order, arrays):
    rows = arrays[0].shape[0]
    outs = [
        jax.ShapeDtypeStruct((3, rows, group.heads * HDIM), jnp.bfloat16)
        for group in groups
        for _ in range(group.peers - 1)
    ]
    blocks = sum(3 * (group.peers - 1) * group.heads for group in groups)
    results = pl.pallas_call(
        functools.partial(pack_body, groups),
        out_shape=outs,
        in_specs=[SMEM, SMEM] + [HBM] * 3,
        out_specs=[HBM] * len(outs),
        scratch_shapes=[pltpu.VMEM((group.peers - 1, 3, rows, group.heads * HDIM), jnp.bfloat16) for group in groups]
        + [pltpu.SemaphoreType.DMA((blocks,)), pltpu.SemaphoreType.DMA((len(outs),))],
        cost_estimate=pl.CostEstimate(flops=0, bytes_accessed=4 * blocks * rows * HDIM, transcendentals=0),
        compiler_params=params(),
        name="pack",
    )(place, order, *arrays)
    sent = []
    for group in groups:
        sent.append(results[: group.peers - 1])
        results = results[group.peers - 1 :]
    return sent


def rows_of(member, rows):
    return pl.ds(pl.multiple_of(member * rows, rows), rows)


def join_body(group, place, order, key_rows, value_rows, *refs):
    peers = group.peers
    pieces, (out, held, own_sems, in_sems, out_sem) = refs[: peers - 1], refs[peers - 1 :]
    me = lax.rem(place[0], peers)
    rows = key_rows.shape[0]
    loads = []
    for which, array in enumerate((key_rows, value_rows)):
        for index in range(group.heads):
            loads.append(
                pltpu.make_async_copy(
                    array.at[:, head_columns(group.head(order, me, index))],
                    held.at[which, rows_of(me, rows), lanes_of(index)],
                    own_sems.at[which, index],
                )
            )
        for shift in range(1, peers):
            source = lax.rem(me + peers - shift, peers)
            loads.append(
                pltpu.make_async_copy(
                    pieces[shift - 1].at[1 + which], held.at[which, rows_of(source, rows)], in_sems.at[shift, which]
                )
            )
    run_copies(loads)
    run_copies([pltpu.make_async_copy(held, out, out_sem)])


def join(group, place, order, key_rows, value_rows, pieces):
    peers, rows = group.peers, key_rows.shape[0]
    shape = (2, peers * rows, group.heads * HDIM)
    return pl.pallas_call(
        functools.partial(join_body, group),
        out_shape=jax.ShapeDtypeStruct(shape, jnp.bfloat16),
        in_specs=[SMEM, SMEM] + [HBM] * (2 + peers - 1),
        out_specs=HBM,
        scratch_shapes=[
            pltpu.VMEM(shape, jnp.bfloat16),
            pltpu.SemaphoreType.DMA((2, group.heads)),
            pltpu.SemaphoreType.DMA((peers, 2)),
            pltpu.SemaphoreType.DMA,
        ],
        cost_estimate=pl.CostEstimate(flops=0, bytes_accessed=4 * shape[0] * shape[1] * shape[2], transcendentals=0),
        compiler_params=params(),
        name="join",
    )(place, order, key_rows, value_rows, *pieces)


def attend_body(group, whole, column, place, order, lists, queries, *refs):
    peers, heads = group.peers, group.heads
    pieces, refs = refs[: peers - 1], refs[peers - 1 :]
    sides, refs = refs[:3], refs[3:]
    outs, refs = refs[:peers], refs[peers:]
    tiles, q_held, kv_held, o_held, scores, peak, total, sums, t_sems, own_sems, q_sems, kv_sems, o_sems = refs
    me = lax.rem(place[0], peers)
    rows = queries.shape[0]
    block = peers * rows
    q_tiles = block // TILE
    first_row = (place[0] // peers) * q_tiles

    heads_dev = lists.shape[0] // whole

    def list_copy(head):
        number = group.head(order, me, head)
        shift = lax.rem(place[0] + whole - number // heads_dev, whole)
        return pltpu.make_async_copy(
            lists.at[shift * heads_dev + lax.rem(number, heads_dev)], tiles.at[head], t_sems.at[head]
        )

    def early(head):
        copies = [
            pltpu.make_async_copy(
                queries.at[:, head_columns(group.head(order, me, head))],
                q_held.at[head, rows_of(me, rows)],
                own_sems.at[head],
            )
        ]
        for shift in range(1, peers):
            source = lax.rem(me + peers - shift, peers)
            copies.append(
                pltpu.make_async_copy(
                    pieces[shift - 1].at[0, :, lanes_of(head)],
                    q_held.at[head, rows_of(source, rows)],
                    q_sems.at[head, shift],
                )
            )
        return copies + sides_of(head, 0)

    def sides_of(head, which):
        return [
            pltpu.make_async_copy(
                sides[side].at[which, :, lanes_of(head)],
                kv_held.at[head, which, pl.ds(side * block, block)],
                kv_sems.at[head, which, side],
            )
            for side in range(3)
        ]

    def back(head):
        return [
            pltpu.make_async_copy(
                o_held.at[head, rows_of(lax.rem(me + shift, peers), rows)],
                outs[shift].at[:, lanes_of(head)],
                o_sems.at[head, shift],
            )
            for shift in range(peers)
        ]

    for head in range(heads):
        for copy in [list_copy(head)] + early(head) + sides_of(head, 1):
            copy.start()

    factor = HDIM ** (-0.5) * LOG2E

    @pl.loop(0, heads)
    def _(head):
        def listed(tile, slot):
            return tiles[head, first_row + tile, column + 1 + slot]

        def live(tile):
            return tiles[head, first_row + tile, column]

        def gathered(which, tile, pair):
            return jnp.concatenate(
                [
                    kv_held[head, which, pl.ds(pl.multiple_of(listed(tile, 2 * pair + half) * TILE, TILE), TILE)]
                    for half in range(2)
                ],
                axis=0,
            )

        list_copy(head).wait()
        longest = live(0)
        for tile in range(1, q_tiles):
            longest = jnp.maximum(longest, live(tile))
        steps = (longest + 1) // 2

        peak[...] = jnp.full_like(peak, -jnp.inf)
        total[...] = jnp.zeros_like(total)
        sums[...] = jnp.zeros_like(sums)
        for copy in early(head):
            copy.wait()

        @pl.loop(0, steps)
        def _(pair):
            for tile in range(q_tiles):
                at = pl.ds(tile * TILE, TILE)
                score = lax.dot_general(
                    q_held[head, at],
                    gathered(0, tile, pair),
                    (((1,), (1,)), ((), ())),
                    preferred_element_type=jnp.float32,
                )
                scores[pair, at] = score
                peak[at] = jnp.maximum(peak[at], jnp.maximum(score[:, :TILE], score[:, TILE:]))

        for tile in range(q_tiles):
            at = pl.ds(tile * TILE, TILE)
            top = jnp.max(peak[at], axis=1, keepdims=True) * factor
            peak[at] = jnp.broadcast_to(top, (TILE, TILE))
        for copy in sides_of(head, 1):
            copy.wait()

        @pl.loop(0, steps)
        def _(pair):
            for tile in range(q_tiles):
                at = pl.ds(tile * TILE, TILE)
                top = peak[at]
                parts = []
                for half in range(2):
                    base = jnp.where(2 * pair + half < live(tile), top, DEAD)
                    parts.append(
                        jnp.exp2(scores[pair, at, pl.ds(half * TILE, TILE)] * factor - base)
                    )
                total[at] += parts[0] + parts[1]
                weight = jnp.concatenate(parts, axis=1).astype(jnp.bfloat16)
                sums[at] += jnp.dot(
                    weight, gathered(1, tile, pair), preferred_element_type=jnp.float32
                )

        for tile in range(q_tiles):
            at = pl.ds(tile * TILE, TILE)
            row_total = jnp.sum(total[at], axis=1, keepdims=True)
            o_held[head, at] = (sums[at] / row_total).astype(jnp.bfloat16)
        for copy in back(head):
            copy.start()

    for head in range(heads):
        for copy in back(head):
            copy.wait()


def attend(group, column, slots, place, order, lists, queries, pieces, sides):
    peers, heads = group.peers, group.heads
    rows = queries.shape[0]
    block = peers * rows
    width = heads * HDIM
    pairs = (slots + 1) // 2
    work = heads * block * slots * TILE
    whole = lax.axis_size("head")
    return pl.pallas_call(
        functools.partial(attend_body, group, whole, column),
        out_shape=[jax.ShapeDtypeStruct((rows, width), jnp.bfloat16)] * peers,
        in_specs=[SMEM, SMEM] + [HBM] * (2 + peers - 1 + 3),
        out_specs=[HBM] * peers,
        scratch_shapes=[
            pltpu.SMEM((heads,) + lists.shape[1:], jnp.int32),
            pltpu.VMEM((heads, block, HDIM), jnp.bfloat16),
            pltpu.VMEM((heads, 2, 3 * block, HDIM), jnp.bfloat16),
            pltpu.VMEM((heads, block, HDIM), jnp.bfloat16),
            pltpu.VMEM((pairs, block, 2 * TILE), jnp.float32),
            pltpu.VMEM((block, TILE), jnp.float32),
            pltpu.VMEM((block, TILE), jnp.float32),
            pltpu.VMEM((block, HDIM), jnp.float32),
            pltpu.SemaphoreType.DMA((heads,)),
            pltpu.SemaphoreType.DMA((heads,)),
            pltpu.SemaphoreType.DMA((heads, peers)),
            pltpu.SemaphoreType.DMA((heads, 2, 3)),
            pltpu.SemaphoreType.DMA((heads, peers)),
        ],
        cost_estimate=pl.CostEstimate(
            flops=4 * work * HDIM, bytes_accessed=8 * block * width * 2, transcendentals=work
        ),
        compiler_params=params(),
        name="attend",
    )(place, order, lists, queries, *pieces, *sides)


def place_body(groups, aliased, place, order, *refs):
    count = sum(group.peers for group in groups)
    pieces, out, held, (in_sems, out_sems) = refs[:count], refs[count + aliased], refs[count + aliased + 1 : -2], refs[-2:]
    loads, stores = [], []
    piece, block = 0, 0
    for number, group in enumerate(groups):
        me = lax.rem(place[0], group.peers)
        for shift in range(group.peers):
            source = lax.rem(me + group.peers - shift, group.peers)
            loads.append(pltpu.make_async_copy(pieces[piece], held[number].at[shift], in_sems.at[piece]))
            copies = []
            for index in range(group.heads):
                copies.append(
                    pltpu.make_async_copy(
                        held[number].at[shift, :, lanes_of(index)],
                        out.at[:, head_columns(group.head(order, source, index))],
                        out_sems.at[block],
                    )
                )
                block += 1
            stores.append(copies)
            piece += 1
    for load in loads:
        load.start()
    for load, copies in zip(loads, stores):
        load.wait()
        for copy in copies:
            copy.start()
    for copies in stores:
        for copy in copies:
            copy.wait()


def place_columns(groups, place, order, pieces, out, shape):
    rows = shape[0]
    aliased = 0 if out is None else 1
    blocks = sum(group.peers * group.heads for group in groups)
    return pl.pallas_call(
        functools.partial(place_body, groups, aliased),
        out_shape=jax.ShapeDtypeStruct(shape, jnp.bfloat16),
        in_specs=[SMEM, SMEM] + [HBM] * (len(pieces) + aliased),
        out_specs=HBM,
        input_output_aliases={2 + len(pieces): 0} if aliased else {},
        scratch_shapes=[pltpu.VMEM((group.peers, rows, group.heads * HDIM), jnp.bfloat16) for group in groups]
        + [
            pltpu.SemaphoreType.DMA((len(pieces),)),
            pltpu.SemaphoreType.DMA((blocks,)),
        ],
        cost_estimate=pl.CostEstimate(flops=0, bytes_accessed=4 * blocks * rows * HDIM, transcendentals=0),
        compiler_params=params(),
        name="place",
    )(place, order, *pieces, *(() if out is None else (out,)))


def around(array, peers, shift):
    count = lax.axis_size("head")
    moves = [(i, i // peers * peers + (i + shift) % peers) for i in range(count)]
    return lax.ppermute(array, "head", moves)


def along(array, shift):
    count = lax.axis_size("ctx")
    return lax.ppermute(array, "ctx", [(i, i + shift) for i in range(count) if 0 <= i + shift < count])


def after(place, values):
    return lax.optimization_barrier((place, values))[0]


def shares(heads, most):
    count = -(-heads // most)
    parts = [heads // count + (i < heads % count) for i in range(count)] if heads else []
    if count > 2 and parts[-1] > 1 and parts[0] == parts[-1]:
        parts[1], parts[-1] = parts[1] + 1, parts[-1] - 1
    return parts


def plan(wide, local, heads_dev, peers):
    half = peers // 2
    base, wides, narrows = 0, [], []
    for heads in shares(wide, WIDE_HEADS):
        wides.append(Group(peers, base, heads))
        base += peers * heads
    for heads in shares((heads_dev * peers - base - local) // half, NARROW_HEADS):
        narrows.append(Group(half, base, heads))
        base += half * heads
    mixed = [Group(1, base, local)] if local else []
    return mixed + narrows[:1] + wides + narrows[1:]


def cases(heads_dev, peers):
    local = heads_dev * peers // 6 // (peers // 2) * (peers // 2)
    return [(-(-heads_dev // 2), local), (-(-2 * heads_dev // 3), local), (heads_dev, 0)]


def list_rows(key_tiles):
    _, cells, slots = key_tiles.shape
    padded = slots + slots % 2
    is_live = key_tiles >= 0
    base = (lax.axis_index("ctx") - 1) * cells
    local_ids = jnp.where(is_live, key_tiles, key_tiles[:, :, :1]) - base
    counts = jnp.sum(is_live.astype(jnp.int32), axis=2, keepdims=True)
    tile = jnp.arange(cells, dtype=jnp.int32)[None, :, None]

    def row(part):
        ids = local_ids // cells * part + local_ids % cells - tile // part * part
        ids = jnp.pad(ids, ((0, 0), (0, 0), (0, padded - slots)))
        ids = jnp.concatenate([counts, ids], axis=2)
        return jnp.pad(ids, ((0, 0), (0, 0), (0, WITHIN - ids.shape[2])))

    peers = lax.axis_size("head")
    rows = [row(cells), row(cells // 2), row(cells // peers)]
    rows = jnp.concatenate(rows, axis=2)
    return jnp.pad(rows, ((0, 0), (0, 0), (0, LANES - rows.shape[2]))).astype(jnp.int32)


def sorted_heads(key_tiles):
    heads_dev, cells, _ = key_tiles.shape
    is_live = key_tiles >= 0
    tile = jnp.arange(cells, dtype=jnp.int32)[None, :, None]

    def leaves(part):
        return jnp.any(is_live & (key_tiles % cells // part != tile // part), axis=(1, 2)).astype(jnp.int32)

    kind = leaves(cells // 2) + leaves(cells // lax.axis_size("head"))
    longest = jnp.max(jnp.sum(is_live.astype(jnp.int32), axis=2), axis=1)
    mine = kind * LANES + longest
    tokens, peers = lax.axis_size("ctx"), lax.axis_size("head")
    spread = jnp.broadcast_to(mine[None], (tokens * peers, heads_dev))
    every = lax.all_to_all(spread, ("ctx", "head"), split_axis=0, concat_axis=0, tiled=True)
    score = jnp.max(every.reshape(tokens, peers * heads_dev), axis=0)
    index = jnp.arange(peers * heads_dev, dtype=jnp.int32)
    ahead = (score[None, :] > score[:, None]) | ((score[None, :] == score[:, None]) & (index[None, :] < index[:, None]))
    rank = jnp.sum(ahead.astype(jnp.int32), axis=1)
    order = jnp.sum(jnp.where(rank[None, :] == index[:, None], index[None, :], 0), axis=1)
    crossing = jnp.sum((score >= 2 * LANES).astype(jnp.int32))
    local = jnp.sum((score < LANES).astype(jnp.int32))
    return order.astype(jnp.int32), crossing, local


def pipeline(groups, slots, place, order, lists, queries, key_rows, value_rows):
    whole = lax.axis_size("head")
    arrays = (queries, key_rows, value_rows)
    packed, arrived, joined, attended = {}, {}, {}, {}
    movers = movers_of(groups)

    def send(index, pieces):
        arrived[index] = [
            around(pieces[shift - 1], groups[index].peers, shift)
            for shift in range(1, groups[index].peers)
        ]

    for kind, index in kernel_order(groups):
        group = groups[index]
        peers = group.peers
        if kind == "pack":
            taken = movers[:AHEAD] if index == movers[0] else movers[AHEAD:]
            results = pack([groups[i] for i in taken], place, order, arrays)
        elif kind == "join":
            results = join(group, place, order, key_rows, value_rows, arrived.get(index, []))
        else:
            column = 0 if peers == whole else 2 * WITHIN if peers == 1 else WITHIN
            results = attend(group, column, slots, place, order, lists, queries, arrived.get(index, []), joined[index])
        if kind == "pack":
            packed.update(zip(taken, results))
        elif kind == "join":
            low, high = (along(results, side) for side in (1, -1))
            joined[index] = (low, results, high)
        else:
            attended[index] = [results[0]] + [around(results[shift], peers, shift) for shift in range(1, peers)]
        for ahead in sent_after(groups, kind, index):
            send(ahead, packed[ahead] if kind == "pack" else after(packed[ahead], results))
        place = after(place, results)
    out = None
    last = len(groups) - 1
    if last:
        pieces = [piece for index in range(last) for piece in attended[index]]
        out = place_columns(groups[:-1], place, order, pieces, out, queries.shape)
    return place_columns(groups[-1:], place, order, attended[last], out, queries.shape)


def gather_heads(rows):
    peers = lax.axis_size("head")
    return jnp.concatenate([rows] + [around(rows, peers, shift) for shift in range(1, peers)], axis=0)


def plans(heads_dev, peers):
    return [plan(wide, local, heads_dev, peers) for wide, local in cases(heads_dev, peers)]


def shards(queries, key_rows, value_rows, key_tiles):
    peers = lax.axis_size("head")
    heads_dev = key_tiles.shape[0]
    place = lax.axis_index("head").astype(jnp.int32).reshape(1)
    lists = gather_heads(list_rows(key_tiles))
    order, crossing, local = sorted_heads(key_tiles)
    which = jnp.int32(len(cases(heads_dev, peers)) - 1)
    for number, (wide, locals_needed) in reversed(list(enumerate(cases(heads_dev, peers)[:-1]))):
        which = jnp.where((crossing <= wide * peers) & (local >= locals_needed), number, which)
    branches = [functools.partial(pipeline, groups, key_tiles.shape[2]) for groups in plans(heads_dev, peers)]
    return lax.switch(which, branches, place, order, lists, queries, key_rows, value_rows)


def movers_of(groups):
    return [index for index, group in enumerate(groups) if group.peers > 1]


def sent_after(groups, kind, index):
    movers = movers_of(groups)
    if index not in movers:
        return []
    number = movers.index(index)
    if kind == "pack":
        return movers[:AHEAD] if number == 0 else []
    if kind == "join":
        return movers[AHEAD : AHEAD + 1] if number == 0 else []
    return movers[number + AHEAD + 1 : number + AHEAD + 2]


def kernel_order(groups):
    movers = movers_of(groups)
    order = [("pack", movers[0])]
    local = groups[0].peers == 1
    if local:
        order.append(("join", 0))
    order += [("pack", index) for index in movers[AHEAD : AHEAD + 1]]
    order.append(("join", movers[0]))
    if local:
        order.append(("attend", 0))
    for index, following in zip(movers, movers[1:] + [None]):
        if following is not None:
            order.append(("join", following))
        order.append(("attend", index))
    return order


def solution(mesh):
    placed = (
        P(("ctx", "head"), None),
        P(("ctx", "head"), None),
        P(("ctx", "head"), None),
        P("head", "ctx", None),
    )
    return jax.shard_map(
        shards, mesh=mesh, in_specs=placed, out_specs=P(("ctx", "head"), None), check_vma=False
    )
```

```python
import functools
from typing import NamedTuple

import jax
import jax.numpy as jnp
from jax import lax
from jax.experimental import pallas as pl
from jax.experimental.pallas import tpu as pltpu
from jax.sharding import PartitionSpec as P


HDIM = 128
TILE = 128
LOG2E = 1.4426950408889634
DEAD = 1e30
AHEAD = 3
VMEM_LIMIT = 67043328
LANES = 128
WITHIN = 32
WIDE_HEADS = 3
NARROW_HEADS = 5


HBM = pl.BlockSpec(memory_space=pl.ANY)
SMEM = pl.BlockSpec(memory_space=pltpu.SMEM)


def run_copies(copies):
    for copy in copies:
        copy.start()
    for copy in copies:
        copy.wait()


def head_columns(head):
    return pl.ds(pl.multiple_of(head * HDIM, HDIM), HDIM)


def lanes_of(index):
    return pl.ds(index * HDIM, HDIM) if isinstance(index, int) else pl.ds(pl.multiple_of(index * HDIM, HDIM), HDIM)


def params():
    return pltpu.CompilerParams(vmem_limit_bytes=VMEM_LIMIT)


class Group(NamedTuple):
    peers: int
    base: int
    heads: int

    def head(self, order, member, index):
        return order[self.base + index * self.peers + member]


def pack_body(groups, place, order, *refs):
    sends = sum(group.peers - 1 for group in groups)
    arrays, outs, held, (in_sems, out_sems) = refs[:3], refs[3 : 3 + sends], refs[3 + sends : -2], refs[-2:]
    loads, stores, block = [], [], 0
    for number, group in enumerate(groups):
        me = lax.rem(place[0], group.peers)
        for shift in range(1, group.peers):
            member = lax.rem(me + shift, group.peers)
            copies = []
            for index in range(group.heads):
                columns = head_columns(group.head(order, member, index))
                for which, array in enumerate(arrays):
                    copies.append(
                        pltpu.make_async_copy(
                            array.at[:, columns],
                            held[number].at[shift - 1, which, :, lanes_of(index)],
                            in_sems.at[block],
                        )
                    )
                    block += 1
            sent = len(loads)
            loads.append(copies)
            stores.append(pltpu.make_async_copy(held[number].at[shift - 1], outs[sent], out_sems.at[sent]))
    for copies in loads:
        for copy in copies:
            copy.start()
    for copies, store in zip(loads, stores):
        for copy in copies:
            copy.wait()
        store.start()
    for store in stores:
        store.wait()


def pack(groups, place, order, arrays):
    rows = arrays[0].shape[0]
    outs = [
        jax.ShapeDtypeStruct((3, rows, group.heads * HDIM), jnp.bfloat16)
        for group in groups
        for _ in range(group.peers - 1)
    ]
    blocks = sum(3 * (group.peers - 1) * group.heads for group in groups)
    results = pl.pallas_call(
        functools.partial(pack_body, groups),
        out_shape=outs,
        in_specs=[SMEM, SMEM] + [HBM] * 3,
        out_specs=[HBM] * len(outs),
        scratch_shapes=[pltpu.VMEM((group.peers - 1, 3, rows, group.heads * HDIM), jnp.bfloat16) for group in groups]
        + [pltpu.SemaphoreType.DMA((blocks,)), pltpu.SemaphoreType.DMA((len(outs),))],
        cost_estimate=pl.CostEstimate(flops=0, bytes_accessed=4 * blocks * rows * HDIM, transcendentals=0),
        compiler_params=params(),
        name="pack",
    )(place, order, *arrays)
    sent = []
    for group in groups:
        sent.append(results[: group.peers - 1])
        results = results[group.peers - 1 :]
    return sent


def rows_of(member, rows):
    return pl.ds(pl.multiple_of(member * rows, rows), rows)


def join_body(group, place, order, key_rows, value_rows, *refs):
    peers = group.peers
    pieces, (out, held, own_sems, in_sems, out_sem) = refs[: peers - 1], refs[peers - 1 :]
    me = lax.rem(place[0], peers)
    rows = key_rows.shape[0]
    loads = []
    for which, array in enumerate((key_rows, value_rows)):
        for index in range(group.heads):
            loads.append(
                pltpu.make_async_copy(
                    array.at[:, head_columns(group.head(order, me, index))],
                    held.at[which, rows_of(me, rows), lanes_of(index)],
                    own_sems.at[which, index],
                )
            )
        for shift in range(1, peers):
            source = lax.rem(me + peers - shift, peers)
            loads.append(
                pltpu.make_async_copy(
                    pieces[shift - 1].at[1 + which], held.at[which, rows_of(source, rows)], in_sems.at[shift, which]
                )
            )
    run_copies(loads)
    run_copies([pltpu.make_async_copy(held, out, out_sem)])


def join(group, place, order, key_rows, value_rows, pieces):
    peers, rows = group.peers, key_rows.shape[0]
    shape = (2, peers * rows, group.heads * HDIM)
    return pl.pallas_call(
        functools.partial(join_body, group),
        out_shape=jax.ShapeDtypeStruct(shape, jnp.bfloat16),
        in_specs=[SMEM, SMEM] + [HBM] * (2 + peers - 1),
        out_specs=HBM,
        scratch_shapes=[
            pltpu.VMEM(shape, jnp.bfloat16),
            pltpu.SemaphoreType.DMA((2, group.heads)),
            pltpu.SemaphoreType.DMA((peers, 2)),
            pltpu.SemaphoreType.DMA,
        ],
        cost_estimate=pl.CostEstimate(flops=0, bytes_accessed=4 * shape[0] * shape[1] * shape[2], transcendentals=0),
        compiler_params=params(),
        name="join",
    )(place, order, key_rows, value_rows, *pieces)


def attend_body(group, whole, column, place, order, lists, queries, *refs):
    peers, heads = group.peers, group.heads
    pieces, refs = refs[: peers - 1], refs[peers - 1 :]
    sides, refs = refs[:3], refs[3:]
    outs, refs = refs[:peers], refs[peers:]
    tiles, q_held, kv_held, o_held, scores, peak, total, sums, t_sems, own_sems, q_sems, kv_sems, o_sems = refs
    me = lax.rem(place[0], peers)
    rows = queries.shape[0]
    block = peers * rows
    q_tiles = block // TILE
    first_row = (place[0] // peers) * q_tiles

    heads_dev = lists.shape[0] // whole

    def list_copy(head):
        number = group.head(order, me, head)
        shift = lax.rem(place[0] + whole - number // heads_dev, whole)
        return pltpu.make_async_copy(
            lists.at[shift * heads_dev + lax.rem(number, heads_dev)], tiles.at[head], t_sems.at[head]
        )

    def early(head):
        copies = [
            pltpu.make_async_copy(
                queries.at[:, head_columns(group.head(order, me, head))],
                q_held.at[head, rows_of(me, rows)],
                own_sems.at[head],
            )
        ]
        for shift in range(1, peers):
            source = lax.rem(me + peers - shift, peers)
            copies.append(
                pltpu.make_async_copy(
                    pieces[shift - 1].at[0, :, lanes_of(head)],
                    q_held.at[head, rows_of(source, rows)],
                    q_sems.at[head, shift],
                )
            )
        return copies + sides_of(head, 0)

    def sides_of(head, which):
        return [
            pltpu.make_async_copy(
                sides[side].at[which, :, lanes_of(head)],
                kv_held.at[head, which, pl.ds(side * block, block)],
                kv_sems.at[head, which, side],
            )
            for side in range(3)
        ]

    def back(head):
        return [
            pltpu.make_async_copy(
                o_held.at[head, rows_of(lax.rem(me + shift, peers), rows)],
                outs[shift].at[:, lanes_of(head)],
                o_sems.at[head, shift],
            )
            for shift in range(peers)
        ]

    for head in range(heads):
        for copy in [list_copy(head)] + early(head) + sides_of(head, 1):
            copy.start()

    factor = HDIM ** (-0.5) * LOG2E

    @pl.loop(0, heads)
    def _(head):
        def listed(tile, slot):
            return tiles[head, first_row + tile, column + 1 + slot]

        def live(tile):
            return tiles[head, first_row + tile, column]

        def gathered(which, tile, pair):
            return jnp.concatenate(
                [
                    kv_held[head, which, pl.ds(pl.multiple_of(listed(tile, 2 * pair + half) * TILE, TILE), TILE)]
                    for half in range(2)
                ],
                axis=0,
            )

        list_copy(head).wait()
        longest = live(0)
        for tile in range(1, q_tiles):
            longest = jnp.maximum(longest, live(tile))
        steps = (longest + 1) // 2

        peak[...] = jnp.full_like(peak, -jnp.inf)
        total[...] = jnp.zeros_like(total)
        sums[...] = jnp.zeros_like(sums)
        for copy in early(head):
            copy.wait()

        @pl.loop(0, steps)
        def _(pair):
            for tile in range(q_tiles):
                at = pl.ds(tile * TILE, TILE)
                score = lax.dot_general(
                    q_held[head, at],
                    gathered(0, tile, pair),
                    (((1,), (1,)), ((), ())),
                    preferred_element_type=jnp.float32,
                )
                scores[pair, at] = score
                peak[at] = jnp.maximum(peak[at], jnp.maximum(score[:, :TILE], score[:, TILE:]))

        for tile in range(q_tiles):
            at = pl.ds(tile * TILE, TILE)
            top = jnp.max(peak[at], axis=1, keepdims=True) * factor
            peak[at] = jnp.broadcast_to(top, (TILE, TILE))
        for copy in sides_of(head, 1):
            copy.wait()

        @pl.loop(0, steps)
        def _(pair):
            for tile in range(q_tiles):
                at = pl.ds(tile * TILE, TILE)
                top = peak[at]
                parts = []
                for half in range(2):
                    base = jnp.where(2 * pair + half < live(tile), top, DEAD)
                    parts.append(
                        jnp.exp2(scores[pair, at, pl.ds(half * TILE, TILE)] * factor - base)
                    )
                total[at] += parts[0] + parts[1]
                weight = jnp.concatenate(parts, axis=1).astype(jnp.bfloat16)
                sums[at] += jnp.dot(
                    weight, gathered(1, tile, pair), preferred_element_type=jnp.float32
                )

        for tile in range(q_tiles):
            at = pl.ds(tile * TILE, TILE)
            row_total = jnp.sum(total[at], axis=1, keepdims=True)
            o_held[head, at] = (sums[at] / row_total).astype(jnp.bfloat16)
        for copy in back(head):
            copy.start()

    for head in range(heads):
        for copy in back(head):
            copy.wait()


def attend(group, column, slots, place, order, lists, queries, pieces, sides):
    peers, heads = group.peers, group.heads
    rows = queries.shape[0]
    block = peers * rows
    width = heads * HDIM
    pairs = (slots + 1) // 2
    work = heads * block * slots * TILE
    whole = lax.axis_size("head")
    return pl.pallas_call(
        functools.partial(attend_body, group, whole, column),
        out_shape=[jax.ShapeDtypeStruct((rows, width), jnp.bfloat16)] * peers,
        in_specs=[SMEM, SMEM] + [HBM] * (2 + peers - 1 + 3),
        out_specs=[HBM] * peers,
        scratch_shapes=[
            pltpu.SMEM((heads,) + lists.shape[1:], jnp.int32),
            pltpu.VMEM((heads, block, HDIM), jnp.bfloat16),
            pltpu.VMEM((heads, 2, 3 * block, HDIM), jnp.bfloat16),
            pltpu.VMEM((heads, block, HDIM), jnp.bfloat16),
            pltpu.VMEM((pairs, block, 2 * TILE), jnp.float32),
            pltpu.VMEM((block, TILE), jnp.float32),
            pltpu.VMEM((block, TILE), jnp.float32),
            pltpu.VMEM((block, HDIM), jnp.float32),
            pltpu.SemaphoreType.DMA((heads,)),
            pltpu.SemaphoreType.DMA((heads,)),
            pltpu.SemaphoreType.DMA((heads, peers)),
            pltpu.SemaphoreType.DMA((heads, 2, 3)),
            pltpu.SemaphoreType.DMA((heads, peers)),
        ],
        cost_estimate=pl.CostEstimate(
            flops=4 * work * HDIM, bytes_accessed=8 * block * width * 2, transcendentals=work
        ),
        compiler_params=params(),
        name="attend",
    )(place, order, lists, queries, *pieces, *sides)


def place_body(groups, aliased, place, order, *refs):
    count = sum(group.peers for group in groups)
    pieces, out, held, (in_sems, out_sems) = refs[:count], refs[count + aliased], refs[count + aliased + 1 : -2], refs[-2:]
    loads, stores = [], []
    piece, block = 0, 0
    for number, group in enumerate(groups):
        me = lax.rem(place[0], group.peers)
        for shift in range(group.peers):
            source = lax.rem(me + group.peers - shift, group.peers)
            loads.append(pltpu.make_async_copy(pieces[piece], held[number].at[shift], in_sems.at[piece]))
            copies = []
            for index in range(group.heads):
                copies.append(
                    pltpu.make_async_copy(
                        held[number].at[shift, :, lanes_of(index)],
                        out.at[:, head_columns(group.head(order, source, index))],
                        out_sems.at[block],
                    )
                )
                block += 1
            stores.append(copies)
            piece += 1
    for load in loads:
        load.start()
    for load, copies in zip(loads, stores):
        load.wait()
        for copy in copies:
            copy.start()
    for copies in stores:
        for copy in copies:
            copy.wait()


def place_columns(groups, place, order, pieces, out, shape):
    rows = shape[0]
    aliased = 0 if out is None else 1
    blocks = sum(group.peers * group.heads for group in groups)
    return pl.pallas_call(
        functools.partial(place_body, groups, aliased),
        out_shape=jax.ShapeDtypeStruct(shape, jnp.bfloat16),
        in_specs=[SMEM, SMEM] + [HBM] * (len(pieces) + aliased),
        out_specs=HBM,
        input_output_aliases={2 + len(pieces): 0} if aliased else {},
        scratch_shapes=[pltpu.VMEM((group.peers, rows, group.heads * HDIM), jnp.bfloat16) for group in groups]
        + [
            pltpu.SemaphoreType.DMA((len(pieces),)),
            pltpu.SemaphoreType.DMA((blocks,)),
        ],
        cost_estimate=pl.CostEstimate(flops=0, bytes_accessed=4 * blocks * rows * HDIM, transcendentals=0),
        compiler_params=params(),
        name="place",
    )(place, order, *pieces, *(() if out is None else (out,)))


def around(array, peers, shift):
    count = lax.axis_size("head")
    moves = [(i, i // peers * peers + (i + shift) % peers) for i in range(count)]
    return lax.ppermute(array, "head", moves)


def along(array, shift):
    count = lax.axis_size("ctx")
    return lax.ppermute(array, "ctx", [(i, i + shift) for i in range(count) if 0 <= i + shift < count])


def after(place, values):
    return lax.optimization_barrier((place, values))[0]


def shares(heads, most):
    count = -(-heads // most)
    parts = [heads // count + (i < heads % count) for i in range(count)] if heads else []
    if count > 2 and parts[-1] > 1 and parts[0] == parts[-1]:
        parts[1], parts[-1] = parts[1] + 1, parts[-1] - 1
    return parts


def plan(wide, local, heads_dev, peers):
    half = peers // 2
    base, wides, narrows = 0, [], []
    for heads in shares(wide, WIDE_HEADS):
        wides.append(Group(peers, base, heads))
        base += peers * heads
    for heads in shares((heads_dev * peers - base - local) // half, NARROW_HEADS):
        narrows.append(Group(half, base, heads))
        base += half * heads
    mixed = [Group(1, base, local)] if local else []
    return mixed + narrows[:1] + wides + narrows[1:]


def cases(heads_dev, peers):
    local = heads_dev * peers // 6 // (peers // 2) * (peers // 2)
    return [(-(-heads_dev // 2), local), (-(-2 * heads_dev // 3), local), (heads_dev, 0)]


def list_rows(key_tiles):
    _, cells, slots = key_tiles.shape
    padded = slots + slots % 2
    is_live = key_tiles >= 0
    base = (lax.axis_index("ctx") - 1) * cells
    local_ids = jnp.where(is_live, key_tiles, key_tiles[:, :, :1]) - base
    counts = jnp.sum(is_live.astype(jnp.int32), axis=2, keepdims=True)
    tile = jnp.arange(cells, dtype=jnp.int32)[None, :, None]

    def row(part):
        ids = local_ids // cells * part + local_ids % cells - tile // part * part
        ids = jnp.pad(ids, ((0, 0), (0, 0), (0, padded - slots)))
        ids = jnp.concatenate([counts, ids], axis=2)
        return jnp.pad(ids, ((0, 0), (0, 0), (0, WITHIN - ids.shape[2])))

    peers = lax.axis_size("head")
    rows = [row(cells), row(cells // 2), row(cells // peers)]
    rows = jnp.concatenate(rows, axis=2)
    return jnp.pad(rows, ((0, 0), (0, 0), (0, LANES - rows.shape[2]))).astype(jnp.int32)


def sorted_heads(key_tiles):
    heads_dev, cells, _ = key_tiles.shape
    is_live = key_tiles >= 0
    tile = jnp.arange(cells, dtype=jnp.int32)[None, :, None]

    def leaves(part):
        return jnp.any(is_live & (key_tiles % cells // part != tile // part), axis=(1, 2)).astype(jnp.int32)

    kind = leaves(cells // 2) + leaves(cells // lax.axis_size("head"))
    longest = jnp.max(jnp.sum(is_live.astype(jnp.int32), axis=2), axis=1)
    mine = kind * LANES + longest
    tokens, peers = lax.axis_size("ctx"), lax.axis_size("head")
    spread = jnp.broadcast_to(mine[None], (tokens * peers, heads_dev))
    every = lax.all_to_all(spread, ("ctx", "head"), split_axis=0, concat_axis=0, tiled=True)
    score = jnp.max(every.reshape(tokens, peers * heads_dev), axis=0)
    index = jnp.arange(peers * heads_dev, dtype=jnp.int32)
    ahead = (score[None, :] > score[:, None]) | ((score[None, :] == score[:, None]) & (index[None, :] < index[:, None]))
    rank = jnp.sum(ahead.astype(jnp.int32), axis=1)
    order = jnp.sum(jnp.where(rank[None, :] == index[:, None], index[None, :], 0), axis=1)
    crossing = jnp.sum((score >= 2 * LANES).astype(jnp.int32))
    local = jnp.sum((score < LANES).astype(jnp.int32))
    return order.astype(jnp.int32), crossing, local


def pipeline(groups, slots, place, order, lists, queries, key_rows, value_rows):
    whole = lax.axis_size("head")
    arrays = (queries, key_rows, value_rows)
    packed, arrived, joined, attended = {}, {}, {}, {}
    movers = movers_of(groups)

    def send(index, pieces):
        arrived[index] = [
            around(pieces[shift - 1], groups[index].peers, shift)
            for shift in range(1, groups[index].peers)
        ]

    for kind, index in kernel_order(groups):
        group = groups[index]
        peers = group.peers
        if kind == "pack":
            taken = movers[:AHEAD] if index == movers[0] else movers[AHEAD:]
            results = pack([groups[i] for i in taken], place, order, arrays)
        elif kind == "join":
            results = join(group, place, order, key_rows, value_rows, arrived.get(index, []))
        else:
            column = 0 if peers == whole else 2 * WITHIN if peers == 1 else WITHIN
            results = attend(group, column, slots, place, order, lists, queries, arrived.get(index, []), joined[index])
        if kind == "pack":
            packed.update(zip(taken, results))
        elif kind == "join":
            low, high = (along(results, side) for side in (1, -1))
            joined[index] = (low, results, high)
        else:
            attended[index] = [results[0]] + [around(results[shift], peers, shift) for shift in range(1, peers)]
        for ahead in sent_after(groups, kind, index):
            send(ahead, packed[ahead] if kind == "pack" else after(packed[ahead], results))
        place = after(place, results)
    out = None
    last = len(groups) - 1
    if last:
        pieces = [piece for index in range(last) for piece in attended[index]]
        out = place_columns(groups[:-1], place, order, pieces, out, queries.shape)
    return place_columns(groups[-1:], place, order, attended[last], out, queries.shape)


def gather_heads(rows):
    peers = lax.axis_size("head")
    return jnp.concatenate([rows] + [around(rows, peers, shift) for shift in range(1, peers)], axis=0)


def plans(heads_dev, peers):
    return [plan(wide, local, heads_dev, peers) for wide, local in cases(heads_dev, peers)]


def shards(queries, key_rows, value_rows, key_tiles):
    peers = lax.axis_size("head")
    heads_dev = key_tiles.shape[0]
    place = lax.axis_index("head").astype(jnp.int32).reshape(1)
    lists = gather_heads(list_rows(key_tiles))
    order, crossing, local = sorted_heads(key_tiles)
    which = jnp.int32(len(cases(heads_dev, peers)) - 1)
    for number, (wide, locals_needed) in reversed(list(enumerate(cases(heads_dev, peers)[:-1]))):
        which = jnp.where((crossing <= wide * peers) & (local >= locals_needed), number, which)
    branches = [functools.partial(pipeline, groups, key_tiles.shape[2]) for groups in plans(heads_dev, peers)]
    return lax.switch(which, branches, place, order, lists, queries, key_rows, value_rows)


def movers_of(groups):
    return [index for index, group in enumerate(groups) if group.peers > 1]


def sent_after(groups, kind, index):
    movers = movers_of(groups)
    if index not in movers:
        return []
    number = movers.index(index)
    if kind == "pack":
        return movers[:AHEAD] if number == 0 else []
    if kind == "join":
        return []
    return movers[number + AHEAD : number + AHEAD + 1]


def kernel_order(groups):
    movers = movers_of(groups)
    order = [("pack", movers[0])]
    local = groups[0].peers == 1
    if local:
        order.append(("join", 0))
    order += [("pack", index) for index in movers[AHEAD : AHEAD + 1]]
    order.append(("join", movers[0]))
    if local:
        order.append(("attend", 0))
    for index, following in zip(movers, movers[1:] + [None]):
        if following is not None:
            order.append(("join", following))
        order.append(("attend", index))
    return order


def solution(mesh):
    placed = (
        P(("ctx", "head"), None),
        P(("ctx", "head"), None),
        P(("ctx", "head"), None),
        P("head", "ctx", None),
    )
    return jax.shard_map(
        shards, mesh=mesh, in_specs=placed, out_specs=P(("ctx", "head"), None), check_vma=False
    )
```
